512 devices in a mesh: tm: 8 (over x, core), rows: 64 (over z, y).
Axes of the slice: x: 4, y: 4, z: 16, core: 2. Of those that a mesh axis runs over, the one named last changes fastest.
Arguments:
- features: bfloat16 [16, 128, 384, 128], P('tm', 'rows'), may hold values from -6 to 6
- conv_in: bfloat16 [3, 3, 3, 128, 128], replicated, may hold values from -0.109375 to 0.109375
- bias_in: float32 [128], replicated, may hold values from -3 to 3
- down_proj: bfloat16 [2, 2, 128, 256], replicated, may hold values from -0.25 to 0.25
- bias_down: float32 [256], replicated, may hold values from -3 to 3
- spatial_w: bfloat16 [3, 3, 256, 256], replicated, may hold values from -0.125 to 0.125
- temporal_w: bfloat16 [3, 256, 256], replicated, may hold values from -0.21875 to 0.21875
- bias_mid: float32 [256], replicated, may hold values from -3 to 3
- norm_gain: float32 [256], replicated, may hold values from 0.1 to 1.9
- latent_proj: bfloat16 [256, 16], replicated, may hold values from -0.375 to 0.375
Outputs:
- latents: float32 [16, 192, 16, 64], P('tm', 'rows')
The draws below stay inside these ranges and needn't reach their ends.
All inputs are finite; a program needn't handle non-finite values.
Results may differ from the reference program's by a relative error of at most 0.013.
Values may be sent and summed in bfloat16 or wider, within the bound.
A program may use at most 64 MiB of HBM per device.

```python
import jax
import jax.numpy as jnp
from jax import lax

C = 128
C2 = 256
ZC = 16
FRAMES = 16
H = 128
W = 384


def steps_of(rng, extent, cuts, smallest, high):
    def one(dim, blocks):
        draws = jax.random.uniform(jax.random.fold_in(jax.random.fold_in(rng, 6), dim), (blocks,), jnp.float32, smallest / len(cuts), high / len(cuts))
        return jnp.repeat(jnp.exp(draws), extent[dim] // blocks).reshape((-1,) + (1,) * (len(extent) - dim - 1))

    loudness = one(*cuts[0])
    for cut in cuts[1:]:
        loudness = loudness * one(*cut)
    return loudness


def scatter_about(key, extent, scale, limit, shards=(), kind=jnp.bfloat16):
    array = jax.random.normal(key, extent, jnp.float32) * scale
    if len(shards) > 0:
        array = steps_of(key, extent, shards, -0.22, 0.18) * array
    return jnp.clip(array, min=-limit, max=limit).astype(kind)


def setup_inputs(seed: int = 0) -> dict:
    seeds = jax.random.split(jax.random.key(seed), 11)
    features = scatter_about(seeds[0], (FRAMES, H, W, C), 1.0, 6.0, ((0, 8), (1, 64)))
    conv_in = scatter_about(seeds[1], (3, 3, 3, C, C), (27 * C) ** -0.5, 0.109375)
    bias_in = scatter_about(seeds[2], (C,), 0.5, 3.0, (), jnp.float32)
    down_proj = scatter_about(seeds[3], (2, 2, C, C2), (4 * C) ** -0.5, 0.25)
    bias_down = scatter_about(seeds[4], (C2,), 0.5, 3.0, (), jnp.float32)
    spatial_w = scatter_about(seeds[5], (3, 3, C2, C2), (9 * C2) ** -0.5, 0.125)
    temporal_w = scatter_about(seeds[6], (3, C2, C2), (3 * C2) ** -0.5, 0.21875)
    bias_mid = scatter_about(seeds[7], (C2,), 0.5, 3.0, (), jnp.float32)
    norm_gain = jnp.clip(1.0 + 0.18 * jax.random.normal(seeds[8], (C2,), jnp.float32), 0.1, 1.9)
    latent_proj = scatter_about(seeds[9], (C2, ZC), C2 ** -0.5, 0.375)
    return {"features": features, "conv_in": conv_in, "bias_in": bias_in, "down_proj": down_proj, "bias_down": bias_down, "spatial_w": spatial_w, "temporal_w": temporal_w, "bias_mid": bias_mid, "norm_gain": norm_gain, "latent_proj": latent_proj}


def reference(features, conv_in, bias_in, down_proj, bias_down, spatial_w, temporal_w, bias_mid, norm_gain, latent_proj):
    high = lax.Precision.HIGHEST
    source = features.astype(jnp.float32)[None]
    conv1 = lax.conv_general_dilated(source, conv_in.astype(jnp.float32), (1, 1, 1), ((2, 0), (1, 1), (1, 1)), dimension_numbers=('NDHWC', 'DHWIO', 'NDHWC'), precision=high)[0]
    hidden = jax.nn.silu(conv1 + bias_in).astype(jnp.bfloat16)
    frames, height, width, chans = hidden.shape
    patches = hidden.reshape(frames, height // 2, 2, width // 2, 2, chans).transpose(0, 1, 3, 2, 4, 5)
    patches = patches.reshape(frames, height // 2, width // 2, 4 * chans).astype(jnp.float32)
    down = (jnp.dot(patches, down_proj.reshape(4 * chans, -1).astype(jnp.float32), precision=high) + bias_down).astype(jnp.bfloat16)
    act = jax.nn.silu(down.astype(jnp.float32)).astype(jnp.bfloat16)
    spatial = lax.conv_general_dilated(act.astype(jnp.float32), spatial_w.astype(jnp.float32), (1, 1), ((1, 1), (1, 1)), dimension_numbers=('NHWC', 'HWIO', 'NHWC'), precision=high).astype(jnp.bfloat16)
    padded = jnp.concatenate([jnp.zeros((2,) + spatial.shape[1:], jnp.bfloat16), spatial], 0).astype(jnp.float32)
    block = down.astype(jnp.float32) + bias_mid
    for step in range(3):
        block = block + jnp.dot(padded[step:step + frames], temporal_w[step].astype(jnp.float32), precision=high)
    scale = lax.rsqrt(lax.optimization_barrier(jnp.mean(block * block, axis=-1, keepdims=True)) + 1e-06)
    normed = (block * scale * norm_gain).astype(jnp.bfloat16)
    latent = jnp.dot(normed.astype(jnp.float32), latent_proj.astype(jnp.float32), precision=high)
    return latent.transpose(0, 2, 3, 1)
```

```python
import functools

import jax
import jax.numpy as jnp
from jax import lax
from jax.experimental import pallas as pl
from jax.experimental.pallas import tpu as pltpu
from jax.sharding import PartitionSpec as P

MESH = pl.DeviceIdType.MESH
F32 = jnp.float32
BF16 = jnp.bfloat16
PAD = 8


def silu(v):
    return v / (1.0 + jnp.exp(-v))


def remote(src, dst, send, recv, axis, peer):
    return pltpu.make_async_remote_copy(
        src_ref=src, dst_ref=dst, send_sem=send, recv_sem=recv, device_id={axis: peer}, device_id_type=MESH
    )


def kernel(
    sections, shards, feat, conv_in, bias_in, down_proj, bias_down, spatial_w, temporal_w, bias_mid, gain, proj_t, out,
    x, w1, w2, w3, w4, acc, act, acc2, sp, down, normed, projs, outbox, inbox,
    load_sem, own_sem, fs_send, fs_recv, as_send, as_recv, ss_send, ss_recv, a2a_send, a2a_recv, ready,
):
    tm, row = lax.axis_index("tm"), lax.axis_index("rows")
    width, lat = feat.shape[2], down.shape[1]
    chans = proj_t.shape[0]
    per = lat // shards
    above, below = lax.rem(row + shards - 1, shards), lax.rem(row + 1, shards)
    later, earlier = lax.rem(tm + 1, sections), lax.rem(tm + sections - 1, sections)
    even = lax.rem(tm, 2) == 0
    has_above, has_below = row > 0, row < shards - 1
    has_prev, has_next = tm > 0, tm < sections - 1

    barrier = pltpu.get_barrier_semaphore()
    for axis, peer in (("rows", above), ("rows", below), ("tm", later), ("tm", earlier)):
        pl.semaphore_signal(barrier, inc=1, device_id={axis: peer}, device_id_type=MESH)

    own = pltpu.make_async_copy(feat, x.at[pl.ds(2, 2), pl.ds(1, 2)], own_sem)
    own.start()
    loads = [
        pltpu.make_async_copy(src, dst, load_sem.at[i])
        for i, (src, dst) in enumerate(((conv_in, w1), (down_proj, w2), (spatial_w, w3), (temporal_w, w4)))
    ]
    for load in loads:
        load.start()

    pl.semaphore_wait(barrier, 4)

    def pair(slot, frame):
        return fs_send.at[slot, frame], fs_recv.at[slot, frame]

    to_next = [remote(feat.at[f], x.at[f, pl.ds(1, 2)], *pair(2, f), "tm", later) for f in range(2)]
    to_below = [remote(feat.at[f, 1], x.at[2 + f, 0], *pair(0, f), "rows", below) for f in range(2)]
    to_above = [remote(feat.at[f, 0], x.at[2 + f, 3], *pair(1, f), "rows", above) for f in range(2)]
    relay_below = [remote(x.at[f, 2], x.at[f, 0], *pair(3, f), "rows", below) for f in range(2)]
    relay_above = [remote(x.at[f, 1], x.at[f, 3], *pair(4, f), "rows", above) for f in range(2)]
    pass_top = [remote(x.at[2 + f, 0], x.at[f, 0], fs_send.at[5, f], fs_recv.at[3, f], "tm", later) for f in range(2)]
    pass_bottom = [remote(x.at[2 + f, 3], x.at[f, 3], fs_send.at[6, f], fs_recv.at[4, f], "tm", later) for f in range(2)]

    for f in range(2):
        pl.when(has_next)(to_next[f].start)
        pl.when(has_below)(to_below[f].start)
        pl.when(has_above)(to_above[f].start)

    step, distance = 0, 1
    while distance <= shards // 4:
        for peer in (lax.rem(row + distance, shards), lax.rem(row + shards - distance, shards)):
            pl.semaphore_signal(ready.at[step], inc=1, device_id={"rows": peer}, device_id_type=MESH)
        if step == 0:
            edge = jnp.zeros((PAD, x.shape[3]), F32)
            for c in range(3):
                for f in range(2):
                    for o in range(2):
                        acc[c, f, o, pl.ds(0, PAD), :] = edge
                        acc[c, f, o, pl.ds(PAD + width, PAD), :] = edge
                    acc2[c, f, pl.ds(0, PAD), :] = jnp.zeros((PAD, acc2.shape[3]), F32)
                    acc2[c, f, pl.ds(PAD + lat, PAD), :] = jnp.zeros((PAD, acc2.shape[3]), F32)
            projs[...] = jnp.zeros(projs.shape, BF16)
            for s in range(2 * per):
                projs[s, pl.ds(chans * s, chans), :] = proj_t[...]

            @pl.when(jnp.logical_not(has_prev))
            def _():
                x[pl.ds(0, 2)] = jnp.zeros((2,) + x.shape[1:], BF16)
                sp[pl.ds(0, 2)] = jnp.zeros((2,) + sp.shape[1:], BF16)

            @pl.when(jnp.logical_not(has_above))
            def _():
                for f in range(4):
                    x[f, 0] = jnp.zeros(x.shape[2:], BF16)
                for f in range(2):
                    act[f, 0] = jnp.zeros(act.shape[2:], BF16)

            @pl.when(jnp.logical_not(has_below))
            def _():
                for f in range(4):
                    x[f, 3] = jnp.zeros(x.shape[2:], BF16)
                for f in range(2):
                    act[f, 2] = jnp.zeros(act.shape[2:], BF16)
        pl.semaphore_wait(ready.at[step], 2)
        step, distance = step + 1, distance * 2

    both = jnp.logical_and
    relays = both(even, has_prev)
    for f in range(2):
        pl.when(has_prev)(to_next[f].wait_recv)
        pl.when(both(relays, has_below))(relay_below[f].start)
        pl.when(both(relays, has_above))(relay_above[f].start)
    for f in range(2):
        pl.when(has_above)(to_below[f].wait_recv)
        pl.when(both(even, has_above))(pass_top[f].start)
        pl.when(has_below)(to_above[f].wait_recv)
        pl.when(both(even, has_below))(pass_bottom[f].start)
    own.wait()
    loads[0].wait()

    def window(frames, o):
        return jnp.concatenate([x[f, o + b] for f in frames for b in range(3)], axis=-1)

    def taps(steps):
        return jnp.concatenate(
            [jnp.concatenate([w1[a, b, c] for c in range(3)], axis=-1) for a in steps for b in range(3)], axis=0
        )

    def conv(f, frames, steps, first):
        weights = taps(steps)
        for o in range(2):
            total = jnp.dot(window(frames, o), weights, preferred_element_type=F32)
            for c in range(3):
                part = total[:, c * 128 : (c + 1) * 128]
                rows = (c, f, o, pl.ds(PAD, width))
                acc[rows] = part if first else acc[rows] + part

    conv(0, (2,), (2,), True)
    conv(1, (2, 3), (1, 2), True)
    for f in range(2):
        pl.when(both(has_prev, has_above))(relay_below[f].wait_recv)
        pl.when(both(has_prev, has_below))(relay_above[f].wait_recv)
    conv(0, (0, 1), (0, 1), False)
    conv(1, (1,), (0,), False)

    loads[1].wait()
    down_w = w2[...].reshape(4 * w2.shape[2], w2.shape[3])
    act_below = [remote(act.at[f, 1], act.at[f, 0], as_send.at[0, f], as_recv.at[0, f], "rows", below) for f in range(2)]
    act_above = [remote(act.at[f, 1], act.at[f, 2], as_send.at[1, f], as_recv.at[1, f], "rows", above) for f in range(2)]
    for f in range(2):
        parts = []
        for o in range(2):
            for b in range(2):
                v = bias_in[...][None, :]
                for c in range(3):
                    v = v + acc[c, f, o, pl.ds(PAD - 1 + b + c, lat, stride=2), :]
                parts.append(silu(v).astype(BF16))
        d = jnp.dot(jnp.concatenate(parts, axis=-1), down_w, preferred_element_type=F32)
        d = (d + bias_down[...][None, :]).astype(BF16)
        down[f] = d
        act[f, 1] = silu(d.astype(F32)).astype(BF16)
        pl.when(has_below)(act_below[f].start)
        pl.when(has_above)(act_above[f].start)

    loads[2].wait()
    to_later = [remote(sp.at[2 + f], sp.at[f], ss_send.at[f], ss_recv.at[f], "tm", later) for f in range(2)]

    def spatial(f, b, first):
        weights = jnp.concatenate([w3[b, c] for c in range(3)], axis=-1)
        total = jnp.dot(act[f, b], weights, preferred_element_type=F32)
        size = w3.shape[3]
        for c in range(3):
            part = total[:, c * size : (c + 1) * size]
            rows = (c, f, pl.ds(PAD, lat))
            acc2[rows] = part if first else acc2[rows] + part

    for f in range(2):
        spatial(f, 1, True)
    for f in range(2):
        pl.when(has_above)(act_below[f].wait_recv)
        spatial(f, 0, False)
        pl.when(has_below)(act_above[f].wait_recv)
        spatial(f, 2, False)
        v = acc2[0, f, pl.ds(PAD - 1, lat), :]
        for c in (1, 2):
            v = v + acc2[c, f, pl.ds(PAD - 1 + c, lat), :]
        sp[2 + f] = v.astype(BF16)
        pl.when(has_next)(to_later[f].start)

    loads[3].wait()

    def mixed(frame, step):
        return jnp.dot(sp[frame], w4[step], preferred_element_type=F32)

    local = [mixed(2, 2), mixed(3, 2) + mixed(2, 1)]
    for f in range(2):
        pl.when(has_prev)(to_later[f].wait_recv)
    half = normed.shape[3]
    for f in range(2):
        block = down[f].astype(F32) + bias_mid[...][None, :] + local[f]
        block = block + (mixed(0, 0) + mixed(1, 1) if f == 0 else mixed(1, 0))
        scale = lax.rsqrt(jnp.mean(block * block, axis=-1, keepdims=True) + 1e-06)
        value = block * scale * gain[...][None, :]
        for h in range(2):
            normed[f, h] = value[:, h * half : (h + 1) * half]

    total = None
    for f in range(2):
        for c in range(per):
            rows = jnp.concatenate(
                [normed[f, h, pl.ds(c, shards, stride=per), :] for h in range(2)], axis=-1
            ).astype(BF16)
            part = lax.dot_general(
                rows, projs[f * per + c], (((1,), (1,)), ((), ())), preferred_element_type=F32
            )
            total = part if total is None else total + part
    outbox[...] = total[:, None, :]

    def token(peer, source):
        return remote(outbox.at[peer], inbox.at[source], a2a_send.at[peer], a2a_recv.at[source], "rows", peer)

    middle = shards // 2
    token(lax.rem(row + middle, shards), row).start()

    def launch(k, carry):
        token(lax.rem(row + middle - k, shards), row).start()
        token(lax.rem(row + middle + k, shards), row).start()
        return carry

    lax.fori_loop(1, middle, launch, 0)
    inbox[row] = outbox[row]

    for f in range(2):
        pl.when(has_next)(to_next[f].wait_send)
        pl.when(has_next)(to_later[f].wait_send)
        for ok, copies in (
            (has_below, (to_below[f], act_below[f])),
            (has_above, (to_above[f], act_above[f])),
            (both(relays, has_below), (relay_below[f],)),
            (both(relays, has_above), (relay_above[f],)),
            (both(even, has_above), (pass_top[f],)),
            (both(even, has_below), (pass_bottom[f],)),
        ):
            for copy in copies:
                pl.when(ok)(copy.wait_send)

    def land(k, carry):
        peer = lax.rem(row + k, shards)
        token(peer, peer).wait_recv()
        return carry

    def leave(k, carry):
        peer = lax.rem(row + k, shards)
        token(peer, peer).wait_send()
        return carry

    lax.fori_loop(1, shards, land, 0)
    out[...] = jnp.transpose(inbox[:, 0, :])[: 2 * per * chans, :]
    lax.fori_loop(1, shards, leave, 0)


def shards_fn(
    sections, shards, features, conv_in, bias_in, down_proj, bias_down, spatial_w, temporal_w, bias_mid, norm_gain, latent_proj
):
    frames, height, width, c1 = features.shape
    lat, c2 = width // 2, down_proj.shape[3]
    chans = latent_proj.shape[1]
    per = lat // shards
    hbm = pl.BlockSpec(memory_space=pl.ANY)
    vmem = pl.BlockSpec(memory_space=pltpu.VMEM)
    dma = pltpu.SemaphoreType.DMA
    tokens = pl.pallas_call(
        functools.partial(kernel, sections, shards),
        out_shape=jax.ShapeDtypeStruct((frames * per * chans, shards), F32),
        in_specs=[hbm, hbm, vmem, hbm, vmem, hbm, hbm, vmem, vmem, vmem],
        out_specs=vmem,
        scratch_shapes=[
            pltpu.VMEM((4, 4, width, c1), BF16),
            pltpu.VMEM(conv_in.shape, BF16),
            pltpu.VMEM(down_proj.shape, BF16),
            pltpu.VMEM(spatial_w.shape, BF16),
            pltpu.VMEM(temporal_w.shape, BF16),
            pltpu.VMEM((3, 2, 2, width + 2 * PAD, c1), F32),
            pltpu.VMEM((2, 3, lat, c2), BF16),
            pltpu.VMEM((3, 2, lat + 2 * PAD, c2), F32),
            pltpu.VMEM((4, lat, c2), BF16),
            pltpu.VMEM((2, lat, c2), BF16),
            pltpu.VMEM((2, 2, lat, c2 // 2), F32),
            pltpu.VMEM((2 * per, 128, c2), BF16),
            pltpu.VMEM((shards, 1, 128), F32),
            pltpu.VMEM((shards, 1, 128), F32),
            dma((4,)),
            dma,
            dma((7, 2)),
            dma((5, 2)),
            dma((2, 2)),
            dma((2, 2)),
            dma((2,)),
            dma((2,)),
            dma((shards,)),
            dma((shards,)),
            pltpu.SemaphoreType.REGULAR((8,)),
        ],
        compiler_params=pltpu.CompilerParams(collective_id=0, has_side_effects=True, vmem_limit_bytes=67_043_328),
        name="encoder",
    )(features, conv_in, bias_in, down_proj, bias_down, spatial_w, temporal_w, bias_mid, norm_gain, latent_proj.T)
    return tokens.reshape(frames, per, chans, shards)


def solution(mesh):
    sizes = mesh.shape
    return jax.shard_map(
        functools.partial(shards_fn, sizes["tm"], sizes["rows"]),
        mesh=mesh,
        in_specs=(P("tm", "rows", None, None), P(), P(), P(), P(), P(), P(), P(), P(), P()),
        out_specs=P("tm", "rows", None, None),
        check_vma=False,
    )
```

```python
import functools

import jax
import jax.numpy as jnp
from jax import lax
from jax.experimental import pallas as pl
from jax.experimental.pallas import tpu as pltpu
from jax.sharding import PartitionSpec as P

MESH = pl.DeviceIdType.MESH
F32 = jnp.float32
BF16 = jnp.bfloat16
PAD = 8


def silu(v):
    return v / (1.0 + jnp.exp(-v))


def remote(src, dst, send, recv, axis, peer):
    return pltpu.make_async_remote_copy(
        src_ref=src, dst_ref=dst, send_sem=send, recv_sem=recv, device_id={axis: peer}, device_id_type=MESH
    )


def kernel(
    sections, shards, feat, conv_in, bias_in_h, down_proj, bias_down_h, spatial_w, temporal_w, bias_mid_h, gain_h, proj_h, out,
    x, w1, w2, w3, w4, bias_in, bias_down, bias_mid, gain, proj_t, acc, act, acc2, sp, down, normed, projs, outbox, inbox,
    load_sem, own_sem, fs_send, fs_recv, as_send, as_recv, ss_send, ss_recv, a2a_send, a2a_recv, ready,
):
    tm, row = lax.axis_index("tm"), lax.axis_index("rows")
    width, lat = feat.shape[2], down.shape[1]
    chans = proj_t.shape[0]
    per = lat // shards
    above, below = lax.rem(row + shards - 1, shards), lax.rem(row + 1, shards)
    later, earlier = lax.rem(tm + 1, sections), lax.rem(tm + sections - 1, sections)
    even = lax.rem(tm, 2) == 0
    has_above, has_below = row > 0, row < shards - 1
    has_prev, has_next = tm > 0, tm < sections - 1

    barrier = pltpu.get_barrier_semaphore()
    for axis, peer in (("rows", above), ("rows", below), ("tm", later), ("tm", earlier)):
        pl.semaphore_signal(barrier, inc=1, device_id={axis: peer}, device_id_type=MESH)

    own = pltpu.make_async_copy(feat, x.at[pl.ds(2, 2), pl.ds(1, 2)], own_sem)
    own.start()
    loads = [
        pltpu.make_async_copy(src, dst, load_sem.at[i])
        for i, (src, dst) in enumerate(
            (
                (conv_in, w1), (down_proj, w2), (spatial_w, w3), (temporal_w, w4), (bias_in_h, bias_in),
                (bias_down_h, bias_down), (bias_mid_h, bias_mid), (gain_h, gain), (proj_h, proj_t),
            )
        )
    ]
    for load in loads:
        load.start()

    edge = jnp.zeros((PAD, x.shape[3]), F32)
    for c in range(3):
        for f in range(2):
            for o in range(2):
                acc[c, f, o, pl.ds(0, PAD), :] = edge
                acc[c, f, o, pl.ds(PAD + width, PAD), :] = edge
            acc2[c, f, pl.ds(0, PAD), :] = jnp.zeros((PAD, acc2.shape[3]), F32)
            acc2[c, f, pl.ds(PAD + lat, PAD), :] = jnp.zeros((PAD, acc2.shape[3]), F32)
    projs[...] = jnp.zeros(projs.shape, BF16)

    @pl.when(jnp.logical_not(has_prev))
    def _():
        x[pl.ds(0, 2)] = jnp.zeros((2,) + x.shape[1:], BF16)
        sp[pl.ds(0, 2)] = jnp.zeros((2,) + sp.shape[1:], BF16)

    @pl.when(jnp.logical_not(has_above))
    def _():
        for f in range(4):
            x[f, 0] = jnp.zeros(x.shape[2:], BF16)
        for f in range(2):
            act[f, 0] = jnp.zeros(act.shape[2:], BF16)

    @pl.when(jnp.logical_not(has_below))
    def _():
        for f in range(4):
            x[f, 3] = jnp.zeros(x.shape[2:], BF16)
        for f in range(2):
            act[f, 2] = jnp.zeros(act.shape[2:], BF16)

    pl.semaphore_wait(barrier, 4)

    def pair(slot, frame):
        return fs_send.at[slot, frame], fs_recv.at[slot, frame]

    to_next = [remote(feat.at[f], x.at[f, pl.ds(1, 2)], *pair(2, f), "tm", later) for f in range(2)]
    to_below = [remote(feat.at[f, 1], x.at[2 + f, 0], *pair(0, f), "rows", below) for f in range(2)]
    to_above = [remote(feat.at[f, 0], x.at[2 + f, 3], *pair(1, f), "rows", above) for f in range(2)]
    relay_below = [remote(x.at[f, 2], x.at[f, 0], *pair(3, f), "rows", below) for f in range(2)]
    relay_above = [remote(x.at[f, 1], x.at[f, 3], *pair(4, f), "rows", above) for f in range(2)]
    pass_top = [remote(x.at[2 + f, 0], x.at[f, 0], fs_send.at[5, f], fs_recv.at[3, f], "tm", later) for f in range(2)]
    pass_bottom = [remote(x.at[2 + f, 3], x.at[f, 3], fs_send.at[6, f], fs_recv.at[4, f], "tm", later) for f in range(2)]

    for f in range(2):
        pl.when(has_next)(to_next[f].start)
        pl.when(has_below)(to_below[f].start)
        pl.when(has_above)(to_above[f].start)

    rounds = []
    while 2 ** len(rounds) <= shards // 4:
        rounds.append(2 ** len(rounds))

    def tell(step):
        if step < len(rounds):
            for peer in (lax.rem(row + rounds[step], shards), lax.rem(row + shards - rounds[step], shards)):
                pl.semaphore_signal(ready.at[step], inc=1, device_id={"rows": peer}, device_id_type=MESH)

    def hear(step):
        if step < len(rounds):
            pl.semaphore_wait(ready.at[step], 2)
            tell(step + 1)

    tell(0)

    def conv(f, frames, kept, first):
        for o in range(2):
            steps = [(n, n - f, b) for n in frames for b in kept[o]]
            lhs = jnp.concatenate([x[n, o + b] for n, a, b in steps], axis=-1)
            rhs = jnp.concatenate(
                [jnp.concatenate([w1[a, b, c] for c in range(3)], axis=-1) for n, a, b in steps], axis=0
            )
            total = jnp.dot(lhs, rhs, preferred_element_type=F32)
            for c in range(3):
                part = total[:, c * 128 : (c + 1) * 128]
                rows = (c, f, o, pl.ds(PAD, width))
                acc[rows] = part if first else acc[rows] + part

    held, halo = ((1, 2), (0, 1)), ((0,), (2,))
    own.wait()
    loads[0].wait()
    conv(0, (2,), held, True)
    conv(1, (2, 3), held, True)
    hear(0)

    both = jnp.logical_and
    relays = both(even, has_prev)
    for f in range(2):
        pl.when(has_prev)(to_next[f].wait_recv)
        pl.when(both(relays, has_below))(relay_below[f].start)
        pl.when(both(relays, has_above))(relay_above[f].start)
        pl.when(has_above)(to_below[f].wait_recv)
        pl.when(both(even, has_above))(pass_top[f].start)
        pl.when(has_below)(to_above[f].wait_recv)
        pl.when(both(even, has_below))(pass_bottom[f].start)
    hear(1)
    conv(0, (0, 1), held, False)
    conv(0, (2,), halo, False)
    hear(2)
    conv(1, (1,), held, False)
    conv(1, (2, 3), halo, False)
    for load in loads[4:]:
        load.wait()
    for s in range(2 * per):
        projs[s, pl.ds(chans * s, chans), :] = proj_t[...]

    loads[1].wait()
    down_w = w2[...].reshape(4 * w2.shape[2], w2.shape[3])
    act_below = [remote(act.at[f, 1], act.at[f, 0], as_send.at[0, f], as_recv.at[0, f], "rows", below) for f in range(2)]
    act_above = [remote(act.at[f, 1], act.at[f, 2], as_send.at[1, f], as_recv.at[1, f], "rows", above) for f in range(2)]
    for f in range(2):
        for n in range(f, 2):
            if n == 0 or f == 0:
                pl.when(both(has_prev, has_above))(relay_below[n].wait_recv)
                pl.when(both(has_prev, has_below))(relay_above[n].wait_recv)
        conv(f, tuple(range(f, 2)), halo, False)
        parts = []
        for o in range(2):
            for b in range(2):
                v = bias_in[...][None, :]
                for c in range(3):
                    v = v + acc[c, f, o, pl.ds(PAD - 1 + b + c, lat, stride=2), :]
                parts.append(silu(v).astype(BF16))
        d = jnp.dot(jnp.concatenate(parts, axis=-1), down_w, preferred_element_type=F32)
        d = (d + bias_down[...][None, :]).astype(BF16)
        down[f] = d
        act[f, 1] = silu(d.astype(F32)).astype(BF16)
        pl.when(has_below)(act_below[f].start)
        pl.when(has_above)(act_above[f].start)

    hear(3)
    loads[2].wait()
    to_later = [remote(sp.at[2 + f], sp.at[f], ss_send.at[f], ss_recv.at[f], "tm", later) for f in range(2)]

    def spatial(f, b, first):
        weights = jnp.concatenate([w3[b, c] for c in range(3)], axis=-1)
        total = jnp.dot(act[f, b], weights, preferred_element_type=F32)
        size = w3.shape[3]
        for c in range(3):
            part = total[:, c * size : (c + 1) * size]
            rows = (c, f, pl.ds(PAD, lat))
            acc2[rows] = part if first else acc2[rows] + part

    for f in range(2):
        spatial(f, 1, True)
    for f in range(2):
        pl.when(has_above)(act_below[f].wait_recv)
        spatial(f, 0, False)
        pl.when(has_below)(act_above[f].wait_recv)
        spatial(f, 2, False)
        v = acc2[0, f, pl.ds(PAD - 1, lat), :]
        for c in (1, 2):
            v = v + acc2[c, f, pl.ds(PAD - 1 + c, lat), :]
        sp[2 + f] = v.astype(BF16)
        pl.when(has_next)(to_later[f].start)

    loads[3].wait()

    def mixed(frame, step):
        return jnp.dot(sp[frame], w4[step], preferred_element_type=F32)

    local = [mixed(2, 2), mixed(3, 2) + mixed(2, 1)]
    for f in range(2):
        pl.when(has_prev)(to_later[f].wait_recv)
    half = normed.shape[3]
    for f in range(2):
        block = down[f].astype(F32) + bias_mid[...][None, :] + local[f]
        block = block + (mixed(0, 0) + mixed(1, 1) if f == 0 else mixed(1, 0))
        scale = lax.rsqrt(jnp.mean(block * block, axis=-1, keepdims=True) + 1e-06)
        value = block * scale * gain[...][None, :]
        for h in range(2):
            normed[f, h] = value[:, h * half : (h + 1) * half]

    total = None
    for f in range(2):
        for c in range(per):
            rows = jnp.concatenate(
                [normed[f, h, pl.ds(c, shards, stride=per), :] for h in range(2)], axis=-1
            ).astype(BF16)
            part = lax.dot_general(
                rows, projs[f * per + c], (((1,), (1,)), ((), ())), preferred_element_type=F32
            )
            total = part if total is None else total + part
    outbox[...] = total[:, None, :]

    hear(4)

    def token(peer, source):
        return remote(outbox.at[peer], inbox.at[source], a2a_send.at[peer], a2a_recv.at[source], "rows", peer)

    middle = shards // 2
    token(lax.rem(row + middle, shards), row).start()

    def launch(k, carry):
        token(lax.rem(row + middle - k, shards), row).start()
        token(lax.rem(row + middle + k, shards), row).start()
        return carry

    lax.fori_loop(1, middle, launch, 0)
    inbox[row] = outbox[row]

    for f in range(2):
        pl.when(has_next)(to_next[f].wait_send)
        pl.when(has_next)(to_later[f].wait_send)
        for ok, copies in (
            (has_below, (to_below[f], act_below[f])),
            (has_above, (to_above[f], act_above[f])),
            (both(relays, has_below), (relay_below[f],)),
            (both(relays, has_above), (relay_above[f],)),
            (both(even, has_above), (pass_top[f],)),
            (both(even, has_below), (pass_bottom[f],)),
        ):
            for copy in copies:
                pl.when(ok)(copy.wait_send)

    def land(k, carry):
        peer = lax.rem(row + k, shards)
        token(peer, peer).wait_recv()
        return carry

    def leave(k, carry):
        peer = lax.rem(row + k, shards)
        token(peer, peer).wait_send()
        return carry

    lax.fori_loop(1, shards, land, 0)
    out[...] = jnp.transpose(inbox[:, 0, :])[: 2 * per * chans, :]
    lax.fori_loop(1, shards, leave, 0)


def shards_fn(
    sections, shards, features, conv_in, bias_in, down_proj, bias_down, spatial_w, temporal_w, bias_mid, norm_gain, latent_proj
):
    frames, height, width, c1 = features.shape
    lat, c2 = width // 2, down_proj.shape[3]
    chans = latent_proj.shape[1]
    per = lat // shards
    hbm = pl.BlockSpec(memory_space=pl.ANY)
    vmem = pl.BlockSpec(memory_space=pltpu.VMEM)
    dma = pltpu.SemaphoreType.DMA
    tokens = pl.pallas_call(
        functools.partial(kernel, sections, shards),
        out_shape=jax.ShapeDtypeStruct((frames * per * chans, shards), F32),
        in_specs=[hbm] * 10,
        out_specs=vmem,
        scratch_shapes=[
            pltpu.VMEM((4, 4, width, c1), BF16),
            pltpu.VMEM(conv_in.shape, BF16),
            pltpu.VMEM(down_proj.shape, BF16),
            pltpu.VMEM(spatial_w.shape, BF16),
            pltpu.VMEM(temporal_w.shape, BF16),
            pltpu.VMEM(bias_in.shape, F32),
            pltpu.VMEM(bias_down.shape, F32),
            pltpu.VMEM(bias_mid.shape, F32),
            pltpu.VMEM(norm_gain.shape, F32),
            pltpu.VMEM(latent_proj.shape[::-1], BF16),
            pltpu.VMEM((3, 2, 2, width + 2 * PAD, c1), F32),
            pltpu.VMEM((2, 3, lat, c2), BF16),
            pltpu.VMEM((3, 2, lat + 2 * PAD, c2), F32),
            pltpu.VMEM((4, lat, c2), BF16),
            pltpu.VMEM((2, lat, c2), BF16),
            pltpu.VMEM((2, 2, lat, c2 // 2), F32),
            pltpu.VMEM((2 * per, 128, c2), BF16),
            pltpu.VMEM((shards, 1, 128), F32),
            pltpu.VMEM((shards, 1, 128), F32),
            dma((9,)),
            dma,
            dma((7, 2)),
            dma((5, 2)),
            dma((2, 2)),
            dma((2, 2)),
            dma((2,)),
            dma((2,)),
            dma((shards,)),
            dma((shards,)),
            pltpu.SemaphoreType.REGULAR((8,)),
        ],
        compiler_params=pltpu.CompilerParams(collective_id=0, has_side_effects=True, vmem_limit_bytes=67_043_328),
        name="encoder",
    )(features, conv_in, bias_in, down_proj, bias_down, spatial_w, temporal_w, bias_mid, norm_gain, latent_proj.T)
    return tokens.reshape(frames, per, chans, shards)


def solution(mesh):
    sizes = mesh.shape
    return jax.shard_map(
        functools.partial(shards_fn, sizes["tm"], sizes["rows"]),
        mesh=mesh,
        in_specs=(P("tm", "rows", None, None), P(), P(), P(), P(), P(), P(), P(), P(), P()),
        out_specs=P("tm", "rows", None, None),
        check_vma=False,
    )
```

```python
import functools

import jax
import jax.numpy as jnp
from jax import lax
from jax.experimental import pallas as pl
from jax.experimental.pallas import tpu as pltpu
from jax.sharding import PartitionSpec as P

MESH = pl.DeviceIdType.MESH
F32 = jnp.float32
BF16 = jnp.bfloat16
PAD = 8


def silu(v):
    return v / (1.0 + jnp.exp(-v))


def remote(src, dst, send, recv, axis, peer):
    return pltpu.make_async_remote_copy(
        src_ref=src, dst_ref=dst, send_sem=send, recv_sem=recv, device_id={axis: peer}, device_id_type=MESH
    )


def kernel(
    sections, shards, feat, conv_in, bias_in_h, down_proj, bias_down_h, spatial_w, temporal_w, bias_mid_h, gain_h, proj_h, out,
    x, w1, w2, w3, w4, bias_in, bias_down, bias_mid, gain, proj_t, acc, act, acc2, sp, down, normed, projs, outbox, inbox,
    load_sem, own_sem, fs_send, fs_recv, as_send, as_recv, ss_send, ss_recv, a2a_send, a2a_recv, ready,
):
    tm, row = lax.axis_index("tm"), lax.axis_index("rows")
    width, lat = feat.shape[2], down.shape[1]
    chans = proj_t.shape[0]
    per = lat // shards
    above, below = lax.rem(row + shards - 1, shards), lax.rem(row + 1, shards)
    later, earlier = lax.rem(tm + 1, sections), lax.rem(tm + sections - 1, sections)
    even = lax.rem(tm, 2) == 0
    has_above, has_below = row > 0, row < shards - 1
    has_prev, has_next = tm > 0, tm < sections - 1

    barrier = pltpu.get_barrier_semaphore()
    for axis, peer in (("rows", above), ("rows", below), ("tm", later), ("tm", earlier)):
        pl.semaphore_signal(barrier, inc=1, device_id={axis: peer}, device_id_type=MESH)

    own = pltpu.make_async_copy(feat, x.at[pl.ds(2, 2), pl.ds(1, 2)], own_sem)
    own.start()
    loads = [
        pltpu.make_async_copy(src, dst, load_sem.at[i])
        for i, (src, dst) in enumerate(
            (
                (conv_in, w1), (down_proj, w2), (spatial_w, w3), (temporal_w, w4), (bias_in_h, bias_in),
                (bias_down_h, bias_down), (bias_mid_h, bias_mid), (gain_h, gain), (proj_h, proj_t),
            )
        )
    ]
    for load in loads:
        load.start()

    edge = jnp.zeros((PAD, x.shape[3]), F32)
    for c in range(3):
        for f in range(2):
            for o in range(2):
                acc[c, f, o, pl.ds(0, PAD), :] = edge
                acc[c, f, o, pl.ds(PAD + width, PAD), :] = edge
            acc2[c, f, pl.ds(0, PAD), :] = jnp.zeros((PAD, acc2.shape[3]), F32)
            acc2[c, f, pl.ds(PAD + lat, PAD), :] = jnp.zeros((PAD, acc2.shape[3]), F32)
    projs[...] = jnp.zeros(projs.shape, BF16)

    @pl.when(jnp.logical_not(has_prev))
    def _():
        x[pl.ds(0, 2)] = jnp.zeros((2,) + x.shape[1:], BF16)
        sp[pl.ds(0, 2)] = jnp.zeros((2,) + sp.shape[1:], BF16)

    @pl.when(jnp.logical_not(has_above))
    def _():
        for f in range(4):
            x[f, 0] = jnp.zeros(x.shape[2:], BF16)
        for f in range(2):
            act[f, 0] = jnp.zeros(act.shape[2:], BF16)

    @pl.when(jnp.logical_not(has_below))
    def _():
        for f in range(4):
            x[f, 3] = jnp.zeros(x.shape[2:], BF16)
        for f in range(2):
            act[f, 2] = jnp.zeros(act.shape[2:], BF16)

    pl.semaphore_wait(barrier, 4)

    def pair(slot, frame):
        return fs_send.at[slot, frame], fs_recv.at[slot, frame]

    to_next = [remote(feat.at[f], x.at[f, pl.ds(1, 2)], *pair(2, f), "tm", later) for f in range(2)]
    to_below = [remote(feat.at[f, 1], x.at[2 + f, 0], *pair(0, f), "rows", below) for f in range(2)]
    to_above = [remote(feat.at[f, 0], x.at[2 + f, 3], *pair(1, f), "rows", above) for f in range(2)]
    relay_below = remote(x.at[1, 2], x.at[1, 0], *pair(3, 1), "rows", below)
    relay_above = remote(x.at[1, 1], x.at[1, 3], *pair(4, 1), "rows", above)
    pass_top = [remote(x.at[2 + f, 0], x.at[f, 0], fs_send.at[5, f], fs_recv.at[3, f], "tm", later) for f in range(2)]
    pass_bottom = [remote(x.at[2 + f, 3], x.at[f, 3], fs_send.at[6, f], fs_recv.at[4, f], "tm", later) for f in range(2)]

    for f in range(2):
        pl.when(has_next)(to_next[1 - f].start)
        pl.when(has_below)(to_below[f].start)
        pl.when(has_above)(to_above[f].start)

    rounds = []
    while 2 ** len(rounds) <= shards // 4:
        rounds.append(2 ** len(rounds))

    def tell(step):
        if step < len(rounds):
            for peer in (lax.rem(row + rounds[step], shards), lax.rem(row + shards - rounds[step], shards)):
                pl.semaphore_signal(ready.at[step], inc=1, device_id={"rows": peer}, device_id_type=MESH)

    def hear(step):
        if step < len(rounds):
            pl.semaphore_wait(ready.at[step], 2)
            tell(step + 1)

    tell(0)

    def conv(f, frames, kept, first):
        for o in range(2):
            steps = [(n, n - f, b) for n in frames for b in kept[o]]
            lhs = jnp.concatenate([x[n, o + b] for n, a, b in steps], axis=-1)
            rhs = jnp.concatenate(
                [jnp.concatenate([w1[a, b, c] for c in range(3)], axis=-1) for n, a, b in steps], axis=0
            )
            total = jnp.dot(lhs, rhs, preferred_element_type=F32)
            for c in range(3):
                part = total[:, c * 128 : (c + 1) * 128]
                rows = (c, f, o, pl.ds(PAD, width))
                acc[rows] = part if first else acc[rows] + part

    held, halo = ((1, 2), (0, 1)), ((0,), (2,))
    own.wait()
    loads[0].wait()
    conv(0, (2,), held, True)
    conv(1, (2, 3), held, True)
    hear(0)

    both = jnp.logical_and
    relays = both(even, has_prev)
    passes = (has_next, even)
    for f in range(2):
        pl.when(has_prev)(to_next[1 - f].wait_recv)
        if f == 0:
            pl.when(both(relays, has_below))(relay_below.start)
            pl.when(both(relays, has_above))(relay_above.start)
        pl.when(has_above)(to_below[f].wait_recv)
        pl.when(both(passes[f], has_above))(pass_top[f].start)
        pl.when(has_below)(to_above[f].wait_recv)
        pl.when(both(passes[f], has_below))(pass_bottom[f].start)
    hear(1)
    conv(1, (1,), held, False)
    conv(1, (2, 3), halo, False)
    hear(2)
    conv(0, (0, 1), held, False)
    conv(0, (2,), halo, False)
    for load in loads[4:]:
        load.wait()
    for s in range(2 * per):
        projs[s, pl.ds(chans * s, chans), :] = proj_t[...]

    loads[1].wait()
    down_w = w2[...].reshape(4 * w2.shape[2], w2.shape[3])
    act_below = [remote(act.at[f, 1], act.at[f, 0], as_send.at[0, f], as_recv.at[0, f], "rows", below) for f in range(2)]
    act_above = [remote(act.at[f, 1], act.at[f, 2], as_send.at[1, f], as_recv.at[1, f], "rows", above) for f in range(2)]
    loads[2].wait()

    def spatial(f, b, first):
        weights = jnp.concatenate([w3[b, c] for c in range(3)], axis=-1)
        total = jnp.dot(act[f, b], weights, preferred_element_type=F32)
        size = w3.shape[3]
        for c in range(3):
            part = total[:, c * size : (c + 1) * size]
            rows = (c, f, pl.ds(PAD, lat))
            acc2[rows] = part if first else acc2[rows] + part

    for f in (1, 0):
        pl.when(both(has_prev, has_above))(pass_top[f].wait_recv)
        pl.when(both(has_prev, has_below))(pass_bottom[f].wait_recv)
        conv(f, tuple(range(f, 2)), halo, False)
        parts = []
        for o in range(2):
            for b in range(2):
                v = bias_in[...][None, :]
                for c in range(3):
                    v = v + acc[c, f, o, pl.ds(PAD - 1 + b + c, lat, stride=2), :]
                parts.append(silu(v).astype(BF16))
        d = jnp.dot(jnp.concatenate(parts, axis=-1), down_w, preferred_element_type=F32)
        d = (d + bias_down[...][None, :]).astype(BF16)
        down[f] = d
        act[f, 1] = silu(d.astype(F32)).astype(BF16)
        pl.when(has_below)(act_below[f].start)
        pl.when(has_above)(act_above[f].start)
        spatial(f, 1, True)

    hear(3)
    to_later = [remote(sp.at[2 + f], sp.at[f], ss_send.at[f], ss_recv.at[f], "tm", later) for f in range(2)]

    for f in (1, 0):
        pl.when(has_above)(act_below[f].wait_recv)
        spatial(f, 0, False)
        pl.when(has_below)(act_above[f].wait_recv)
        spatial(f, 2, False)
        v = acc2[0, f, pl.ds(PAD - 1, lat), :]
        for c in (1, 2):
            v = v + acc2[c, f, pl.ds(PAD - 1 + c, lat), :]
        sp[2 + f] = v.astype(BF16)
        pl.when(has_next)(to_later[f].start)

    loads[3].wait()

    def mixed(frame, step):
        return jnp.dot(sp[frame], w4[step], preferred_element_type=F32)

    local = [mixed(2, 2), mixed(3, 2) + mixed(2, 1)]
    half = normed.shape[3]
    total = None
    for f in (1, 0):
        pl.when(has_prev)(to_later[f].wait_recv)
        block = down[f].astype(F32) + bias_mid[...][None, :] + local[f]
        block = block + (mixed(0, 0) + mixed(1, 1) if f == 0 else mixed(1, 0))
        scale = lax.rsqrt(jnp.mean(block * block, axis=-1, keepdims=True) + 1e-06)
        value = block * scale * gain[...][None, :]
        for h in range(2):
            normed[f, h] = value[:, h * half : (h + 1) * half]
        for c in range(per):
            rows = jnp.concatenate(
                [normed[f, h, pl.ds(c, shards, stride=per), :] for h in range(2)], axis=-1
            ).astype(BF16)
            part = lax.dot_general(
                rows, projs[f * per + c], (((1,), (1,)), ((), ())), preferred_element_type=F32
            )
            total = part if total is None else total + part
    outbox[...] = total[:, None, :]

    hear(4)

    def token(peer, source):
        return remote(outbox.at[peer], inbox.at[source], a2a_send.at[peer], a2a_recv.at[source], "rows", peer)

    middle = shards // 2
    token(lax.rem(row + middle, shards), row).start()

    def launch(k, carry):
        token(lax.rem(row + middle - k, shards), row).start()
        token(lax.rem(row + middle + k, shards), row).start()
        return carry

    lax.fori_loop(1, middle, launch, 0)
    inbox[row] = outbox[row]

    for f in range(2):
        pl.when(has_next)(to_next[f].wait_send)
        pl.when(has_next)(to_later[f].wait_send)
        for ok, copies in (
            (has_below, (to_below[f], act_below[f])),
            (has_above, (to_above[f], act_above[f])),
            (both(relays, has_below), (relay_below,) * f),
            (both(relays, has_above), (relay_above,) * f),
            (both(passes[f], has_above), (pass_top[f],)),
            (both(passes[f], has_below), (pass_bottom[f],)),
        ):
            for copy in copies:
                pl.when(ok)(copy.wait_send)

    def land(k, carry):
        peer = lax.rem(row + k, shards)
        token(peer, peer).wait_recv()
        return carry

    def leave(k, carry):
        peer = lax.rem(row + k, shards)
        token(peer, peer).wait_send()
        return carry

    lax.fori_loop(1, shards, land, 0)
    out[...] = jnp.transpose(inbox[:, 0, :])[: 2 * per * chans, :]
    lax.fori_loop(1, shards, leave, 0)


def shards_fn(
    sections, shards, features, conv_in, bias_in, down_proj, bias_down, spatial_w, temporal_w, bias_mid, norm_gain, latent_proj
):
    frames, height, width, c1 = features.shape
    lat, c2 = width // 2, down_proj.shape[3]
    chans = latent_proj.shape[1]
    per = lat // shards
    hbm = pl.BlockSpec(memory_space=pl.ANY)
    vmem = pl.BlockSpec(memory_space=pltpu.VMEM)
    dma = pltpu.SemaphoreType.DMA
    tokens = pl.pallas_call(
        functools.partial(kernel, sections, shards),
        out_shape=jax.ShapeDtypeStruct((frames * per * chans, shards), F32),
        in_specs=[hbm] * 10,
        out_specs=vmem,
        scratch_shapes=[
            pltpu.VMEM((4, 4, width, c1), BF16),
            pltpu.VMEM(conv_in.shape, BF16),
            pltpu.VMEM(down_proj.shape, BF16),
            pltpu.VMEM(spatial_w.shape, BF16),
            pltpu.VMEM(temporal_w.shape, BF16),
            pltpu.VMEM(bias_in.shape, F32),
            pltpu.VMEM(bias_down.shape, F32),
            pltpu.VMEM(bias_mid.shape, F32),
            pltpu.VMEM(norm_gain.shape, F32),
            pltpu.VMEM(latent_proj.shape[::-1], BF16),
            pltpu.VMEM((3, 2, 2, width + 2 * PAD, c1), F32),
            pltpu.VMEM((2, 3, lat, c2), BF16),
            pltpu.VMEM((3, 2, lat + 2 * PAD, c2), F32),
            pltpu.VMEM((4, lat, c2), BF16),
            pltpu.VMEM((2, lat, c2), BF16),
            pltpu.VMEM((2, 2, lat, c2 // 2), F32),
            pltpu.VMEM((2 * per, 128, c2), BF16),
            pltpu.VMEM((shards, 1, 128), F32),
            pltpu.VMEM((shards, 1, 128), F32),
            dma((9,)),
            dma,
            dma((7, 2)),
            dma((5, 2)),
            dma((2, 2)),
            dma((2, 2)),
            dma((2,)),
            dma((2,)),
            dma((shards,)),
            dma((shards,)),
            pltpu.SemaphoreType.REGULAR((8,)),
        ],
        compiler_params=pltpu.CompilerParams(collective_id=0, has_side_effects=True, vmem_limit_bytes=67_043_328),
        name="encoder",
    )(features, conv_in, bias_in, down_proj, bias_down, spatial_w, temporal_w, bias_mid, norm_gain, latent_proj.T)
    return tokens.reshape(frames, per, chans, shards)


def solution(mesh):
    sizes = mesh.shape
    return jax.shard_map(
        functools.partial(shards_fn, sizes["tm"], sizes["rows"]),
        mesh=mesh,
        in_specs=(P("tm", "rows", None, None), P(), P(), P(), P(), P(), P(), P(), P(), P()),
        out_specs=P("tm", "rows", None, None),
        check_vma=False,
    )
```

```python
import functools

import jax
import jax.numpy as jnp
from jax import lax
from jax.experimental import pallas as pl
from jax.experimental.pallas import tpu as pltpu
from jax.sharding import PartitionSpec as P

MESH = pl.DeviceIdType.MESH
F32 = jnp.float32
BF16 = jnp.bfloat16
PAD = 8


def silu(v):
    return v / (1.0 + jnp.exp(-v))


def remote(src, dst, send, recv, axis, peer):
    return pltpu.make_async_remote_copy(
        src_ref=src, dst_ref=dst, send_sem=send, recv_sem=recv, device_id={axis: peer}, device_id_type=MESH
    )


def kernel(
    sections, shards, feat, conv_in, bias_in_h, down_proj, bias_down_h, spatial_w, temporal_w, bias_mid_h, gain_h, proj_h, out,
    x, w1, w2, w3, w4, bias_in, bias_down, bias_mid, gain, proj_t, acc, act, acc2, sp, down, normed, projs, outbox, inbox,
    load_sem, own_sem, fs_send, fs_recv, as_send, as_recv, ss_send, ss_recv, a2a_send, a2a_recv, ready,
):
    tm, row = lax.axis_index("tm"), lax.axis_index("rows")
    width, lat = feat.shape[2], down.shape[1]
    chans = proj_t.shape[0]
    per = lat // shards
    above, below = lax.rem(row + shards - 1, shards), lax.rem(row + 1, shards)
    later, earlier = lax.rem(tm + 1, sections), lax.rem(tm + sections - 1, sections)
    even = lax.rem(tm, 2) == 0
    has_above, has_below = row > 0, row < shards - 1
    has_prev, has_next = tm > 0, tm < sections - 1

    barrier = pltpu.get_barrier_semaphore()
    for axis, peer in (("rows", above), ("rows", below), ("tm", later), ("tm", earlier)):
        pl.semaphore_signal(barrier, inc=1, device_id={axis: peer}, device_id_type=MESH)

    own = pltpu.make_async_copy(feat, x.at[pl.ds(2, 2), pl.ds(1, 2)], own_sem)
    own.start()
    loads = [
        pltpu.make_async_copy(src, dst, load_sem.at[i])
        for i, (src, dst) in enumerate(
            (
                (conv_in, w1), (down_proj, w2), (spatial_w, w3), (temporal_w, w4), (bias_in_h, bias_in),
                (bias_down_h, bias_down), (bias_mid_h, bias_mid), (gain_h, gain), (proj_h, proj_t),
            )
        )
    ]
    for load in loads:
        load.start()

    edge = jnp.zeros((PAD, x.shape[3]), F32)
    for c in range(3):
        for f in range(2):
            for o in range(2):
                acc[c, f, o, pl.ds(0, PAD), :] = edge
                acc[c, f, o, pl.ds(PAD + width, PAD), :] = edge
            acc2[c, f, pl.ds(0, PAD), :] = jnp.zeros((PAD, acc2.shape[3]), F32)
            acc2[c, f, pl.ds(PAD + lat, PAD), :] = jnp.zeros((PAD, acc2.shape[3]), F32)
    projs[...] = jnp.zeros(projs.shape, BF16)

    @pl.when(jnp.logical_not(has_prev))
    def _():
        x[pl.ds(0, 2)] = jnp.zeros((2,) + x.shape[1:], BF16)
        sp[pl.ds(0, 2)] = jnp.zeros((2,) + sp.shape[1:], BF16)

    @pl.when(jnp.logical_not(has_above))
    def _():
        for f in range(4):
            x[f, 0] = jnp.zeros(x.shape[2:], BF16)
        for f in range(2):
            act[f, 0] = jnp.zeros(act.shape[2:], BF16)

    @pl.when(jnp.logical_not(has_below))
    def _():
        for f in range(4):
            x[f, 3] = jnp.zeros(x.shape[2:], BF16)
        for f in range(2):
            act[f, 2] = jnp.zeros(act.shape[2:], BF16)

    pl.semaphore_wait(barrier, 4)

    def pair(slot, frame):
        return fs_send.at[slot, frame], fs_recv.at[slot, frame]

    to_next = [remote(feat.at[f], x.at[f, pl.ds(1, 2)], *pair(2, f), "tm", later) for f in range(2)]
    to_below = [remote(feat.at[f, 1], x.at[2 + f, 0], *pair(0, f), "rows", below) for f in range(2)]
    to_above = [remote(feat.at[f, 0], x.at[2 + f, 3], *pair(1, f), "rows", above) for f in range(2)]
    relay_below = remote(x.at[1, 2], x.at[1, 0], *pair(3, 1), "rows", below)
    relay_above = remote(x.at[1, 1], x.at[1, 3], *pair(4, 1), "rows", above)
    pass_top = [remote(x.at[2 + f, 0], x.at[f, 0], fs_send.at[5, f], fs_recv.at[3, f], "tm", later) for f in range(2)]
    pass_bottom = [remote(x.at[2 + f, 3], x.at[f, 3], fs_send.at[6, f], fs_recv.at[4, f], "tm", later) for f in range(2)]

    for f in range(2):
        pl.when(has_next)(to_next[1 - f].start)
        pl.when(has_below)(to_below[f].start)
        pl.when(has_above)(to_above[f].start)

    rounds = []
    while 2 ** len(rounds) <= shards // 4:
        rounds.append(2 ** len(rounds))

    def tell(step):
        if step < len(rounds):
            for peer in (lax.rem(row + rounds[step], shards), lax.rem(row + shards - rounds[step], shards)):
                pl.semaphore_signal(ready.at[step], inc=1, device_id={"rows": peer}, device_id_type=MESH)

    def hear(step):
        if step < len(rounds):
            pl.semaphore_wait(ready.at[step], 2)
            tell(step + 1)

    tell(0)

    def conv(f, frames, kept, first):
        for o in range(2):
            steps = [(n, n - f, b) for n in frames for b in kept[o]]
            lhs = jnp.concatenate([x[n, o + b] for n, a, b in steps], axis=-1)
            rhs = jnp.concatenate(
                [jnp.concatenate([w1[a, b, c] for c in range(3)], axis=-1) for n, a, b in steps], axis=0
            )
            total = jnp.dot(lhs, rhs, preferred_element_type=F32)
            for c in range(3):
                part = total[:, c * 128 : (c + 1) * 128]
                rows = (c, f, o, pl.ds(PAD, width))
                acc[rows] = part if first else acc[rows] + part

    held, halo = ((1, 2), (0, 1)), ((0,), (2,))
    own.wait()
    loads[0].wait()
    conv(0, (2,), held, True)
    conv(1, (2, 3), held, True)
    hear(0)

    both = jnp.logical_and
    relays = both(even, has_prev)
    passes = (has_next, even)
    for f in range(2):
        pl.when(has_prev)(to_next[1 - f].wait_recv)
        if f == 0:
            pl.when(both(relays, has_below))(relay_below.start)
            pl.when(both(relays, has_above))(relay_above.start)
        pl.when(has_above)(to_below[f].wait_recv)
        pl.when(both(passes[f], has_above))(pass_top[f].start)
        pl.when(has_below)(to_above[f].wait_recv)
        pl.when(both(passes[f], has_below))(pass_bottom[f].start)
    hear(1)
    conv(1, (1,), held, False)
    conv(1, (2, 3), halo, False)
    hear(2)
    conv(0, (0, 1), held, False)
    conv(0, (2,), halo, False)
    for load in loads[4:]:
        load.wait()
    for s in range(2 * per):
        projs[s, pl.ds(chans * s, chans), :] = proj_t[...]

    loads[1].wait()
    down_w = w2[...].reshape(4 * w2.shape[2], w2.shape[3])
    act_below = [remote(act.at[f, 1], act.at[f, 0], as_send.at[0, f], as_recv.at[0, f], "rows", below) for f in range(2)]
    act_above = [remote(act.at[f, 1], act.at[f, 2], as_send.at[1, f], as_recv.at[1, f], "rows", above) for f in range(2)]
    loads[2].wait()

    def spatial(f, b, first):
        weights = jnp.concatenate([w3[b, c] for c in range(3)], axis=-1)
        total = jnp.dot(act[f, b], weights, preferred_element_type=F32)
        size = w3.shape[3]
        for c in range(3):
            part = total[:, c * size : (c + 1) * size]
            rows = (c, f, pl.ds(PAD, lat))
            acc2[rows] = part if first else acc2[rows] + part

    for f in (1, 0):
        pl.when(both(has_prev, has_above))(pass_top[f].wait_recv)
        pl.when(both(has_prev, has_below))(pass_bottom[f].wait_recv)
        conv(f, tuple(range(f, 2)), halo, False)
        parts = []
        for o in range(2):
            for b in range(2):
                v = bias_in[...][None, :]
                for c in range(3):
                    v = v + acc[c, f, o, pl.ds(PAD - 1 + b + c, lat, stride=2), :]
                parts.append(silu(v).astype(BF16))
        d = jnp.dot(jnp.concatenate(parts, axis=-1), down_w, preferred_element_type=F32)
        d = (d + bias_down[...][None, :]).astype(BF16)
        down[f] = d
        act[f, 1] = silu(d.astype(F32)).astype(BF16)
        pl.when(has_below)(act_below[f].start)
        pl.when(has_above)(act_above[f].start)
        spatial(f, 1, True)

    hear(3)
    to_later = [remote(sp.at[2 + f], sp.at[f], ss_send.at[f], ss_recv.at[f], "tm", later) for f in range(2)]

    for f in (1, 0):
        pl.when(has_above)(act_below[f].wait_recv)
        spatial(f, 0, False)
        pl.when(has_below)(act_above[f].wait_recv)
        spatial(f, 2, False)
        v = acc2[0, f, pl.ds(PAD - 1, lat), :]
        for c in (1, 2):
            v = v + acc2[c, f, pl.ds(PAD - 1 + c, lat), :]
        sp[2 + f] = v.astype(BF16)
        pl.when(has_next)(to_later[f].start)

    loads[3].wait()

    def mixed(frame, step):
        return jnp.dot(sp[frame], w4[step], preferred_element_type=F32)

    local = [mixed(2, 2), mixed(3, 2) + mixed(2, 1)]
    half = normed.shape[3]
    total = None
    for f in (1, 0):
        pl.when(has_prev)(to_later[f].wait_recv)
        block = down[f].astype(F32) + bias_mid[...][None, :] + local[f]
        block = block + (mixed(0, 0) + mixed(1, 1) if f == 0 else mixed(1, 0))
        scale = lax.rsqrt(jnp.mean(block * block, axis=-1, keepdims=True) + 1e-06)
        value = block * scale * gain[...][None, :]
        for h in range(2):
            normed[f, h] = value[:, h * half : (h + 1) * half]
        for c in range(per):
            rows = jnp.concatenate(
                [normed[f, h, pl.ds(c, shards, stride=per), :] for h in range(2)], axis=-1
            ).astype(BF16)
            part = lax.dot_general(
                rows, projs[f * per + c], (((1,), (1,)), ((), ())), preferred_element_type=F32
            )
            total = part if total is None else total + part
    outbox[...] = total[:, None, :]

    hear(4)

    def token(peer, source):
        return remote(outbox.at[peer], inbox.at[source], a2a_send, a2a_recv, "rows", peer)

    middle = shards // 2
    token(lax.rem(row + middle, shards), row).start()

    def launch(k, carry):
        token(lax.rem(row + middle - k, shards), row).start()
        token(lax.rem(row + middle + k, shards), row).start()
        return carry

    lax.fori_loop(1, middle, launch, 0)
    inbox[row] = outbox[row]

    for f in range(2):
        pl.when(has_next)(to_next[f].wait_send)
        pl.when(has_next)(to_later[f].wait_send)
        for ok, copies in (
            (has_below, (to_below[f], act_below[f])),
            (has_above, (to_above[f], act_above[f])),
            (both(relays, has_below), (relay_below,) * f),
            (both(relays, has_above), (relay_above,) * f),
            (both(passes[f], has_above), (pass_top[f],)),
            (both(passes[f], has_below), (pass_bottom[f],)),
        ):
            for copy in copies:
                pl.when(ok)(copy.wait_send)

    others = pl.ds(0, shards - 1)
    pltpu.make_async_copy(outbox.at[others], inbox.at[others], a2a_recv).wait()
    out[...] = jnp.transpose(inbox[:, 0, :])[: 2 * per * chans, :]
    pltpu.make_async_copy(outbox.at[others], inbox.at[others], a2a_send).wait()


def shards_fn(
    sections, shards, features, conv_in, bias_in, down_proj, bias_down, spatial_w, temporal_w, bias_mid, norm_gain, latent_proj
):
    frames, height, width, c1 = features.shape
    lat, c2 = width // 2, down_proj.shape[3]
    chans = latent_proj.shape[1]
    per = lat // shards
    hbm = pl.BlockSpec(memory_space=pl.ANY)
    vmem = pl.BlockSpec(memory_space=pltpu.VMEM)
    dma = pltpu.SemaphoreType.DMA
    tokens = pl.pallas_call(
        functools.partial(kernel, sections, shards),
        out_shape=jax.ShapeDtypeStruct((frames * per * chans, shards), F32),
        in_specs=[hbm] * 10,
        out_specs=vmem,
        scratch_shapes=[
            pltpu.VMEM((4, 4, width, c1), BF16),
            pltpu.VMEM(conv_in.shape, BF16),
            pltpu.VMEM(down_proj.shape, BF16),
            pltpu.VMEM(spatial_w.shape, BF16),
            pltpu.VMEM(temporal_w.shape, BF16),
            pltpu.VMEM(bias_in.shape, F32),
            pltpu.VMEM(bias_down.shape, F32),
            pltpu.VMEM(bias_mid.shape, F32),
            pltpu.VMEM(norm_gain.shape, F32),
            pltpu.VMEM(latent_proj.shape[::-1], BF16),
            pltpu.VMEM((3, 2, 2, width + 2 * PAD, c1), F32),
            pltpu.VMEM((2, 3, lat, c2), BF16),
            pltpu.VMEM((3, 2, lat + 2 * PAD, c2), F32),
            pltpu.VMEM((4, lat, c2), BF16),
            pltpu.VMEM((2, lat, c2), BF16),
            pltpu.VMEM((2, 2, lat, c2 // 2), F32),
            pltpu.VMEM((2 * per, 128, c2), BF16),
            pltpu.VMEM((shards, 1, 128), F32),
            pltpu.VMEM((shards, 1, 128), F32),
            dma((9,)),
            dma,
            dma((7, 2)),
            dma((5, 2)),
            dma((2, 2)),
            dma((2, 2)),
            dma((2,)),
            dma((2,)),
            dma,
            dma,
            pltpu.SemaphoreType.REGULAR((8,)),
        ],
        compiler_params=pltpu.CompilerParams(collective_id=0, has_side_effects=True, vmem_limit_bytes=67_043_328),
        name="encoder",
    )(features, conv_in, bias_in, down_proj, bias_down, spatial_w, temporal_w, bias_mid, norm_gain, latent_proj.T)
    return tokens.reshape(frames, per, chans, shards)


def solution(mesh):
    sizes = mesh.shape
    return jax.shard_map(
        functools.partial(shards_fn, sizes["tm"], sizes["rows"]),
        mesh=mesh,
        in_specs=(P("tm", "rows", None, None), P(), P(), P(), P(), P(), P(), P(), P(), P()),
        out_specs=P("tm", "rows", None, None),
        check_vma=False,
    )
```

```python
import functools

import jax
import jax.numpy as jnp
from jax import lax
from jax.experimental import pallas as pl
from jax.experimental.pallas import tpu as pltpu
from jax.sharding import PartitionSpec as P

MESH = pl.DeviceIdType.MESH
F32 = jnp.float32
BF16 = jnp.bfloat16
PAD = 8


def silu(v):
    return v / (1.0 + jnp.exp(-v))


def remote(src, dst, send, recv, axis, peer):
    return pltpu.make_async_remote_copy(
        src_ref=src, dst_ref=dst, send_sem=send, recv_sem=recv, device_id={axis: peer}, device_id_type=MESH
    )


def kernel(
    sections, shards, feat, conv_in, bias_in_h, down_proj, bias_down_h, spatial_w, temporal_w, bias_mid_h, gain_h, proj_h, out,
    x, w1, w2, w3, w4, bias_in, bias_down, bias_mid, gain, proj_t, acc, act, acc2, sp, down, normed, projs, outbox, inbox,
    load_sem, own_sem, fs_send, fs_recv, as_send, as_recv, ss_send, ss_recv, a2a_send, a2a_recv, ready,
):
    tm, row = lax.axis_index("tm"), lax.axis_index("rows")
    width, lat = feat.shape[2], down.shape[1]
    chans = proj_t.shape[0]
    per = lat // shards
    above, below = lax.rem(row + shards - 1, shards), lax.rem(row + 1, shards)
    later, earlier = lax.rem(tm + 1, sections), lax.rem(tm + sections - 1, sections)
    even = lax.rem(tm, 2) == 0
    has_above, has_below = row > 0, row < shards - 1
    has_prev, has_next = tm > 0, tm < sections - 1

    barrier = pltpu.get_barrier_semaphore()
    for axis, peer in (("rows", above), ("rows", below), ("tm", later), ("tm", earlier)):
        pl.semaphore_signal(barrier, inc=1, device_id={axis: peer}, device_id_type=MESH)

    pl.semaphore_wait(barrier, 4)

    def pair(slot, frame):
        return fs_send.at[slot, frame], fs_recv.at[slot, frame]

    to_next = [remote(feat.at[f], x.at[f, pl.ds(1, 2)], *pair(2, f), "tm", later) for f in range(2)]
    to_below = [remote(feat.at[f, 1], x.at[2 + f, 0], *pair(0, f), "rows", below) for f in range(2)]
    to_above = [remote(feat.at[f, 0], x.at[2 + f, 3], *pair(1, f), "rows", above) for f in range(2)]
    relay_below = remote(x.at[1, 2], x.at[1, 0], *pair(3, 1), "rows", below)
    relay_above = remote(x.at[1, 1], x.at[1, 3], *pair(4, 1), "rows", above)
    pass_top = [remote(x.at[2 + f, 0], x.at[f, 0], fs_send.at[5, f], fs_recv.at[3, f], "tm", later) for f in range(2)]
    pass_bottom = [remote(x.at[2 + f, 3], x.at[f, 3], fs_send.at[6, f], fs_recv.at[4, f], "tm", later) for f in range(2)]

    for f in range(2):
        pl.when(has_next)(to_next[1 - f].start)
        pl.when(has_below)(to_below[f].start)
        pl.when(has_above)(to_above[f].start)

    rounds = []
    while 2 ** len(rounds) <= shards // 4:
        rounds.append(2 ** len(rounds))

    def tell(step):
        if step < len(rounds):
            for peer in (lax.rem(row + rounds[step], shards), lax.rem(row + shards - rounds[step], shards)):
                pl.semaphore_signal(ready.at[step], inc=1, device_id={"rows": peer}, device_id_type=MESH)

    def hear(step):
        if step < len(rounds):
            pl.semaphore_wait(ready.at[step], 2)
            tell(step + 1)

    tell(0)

    own = pltpu.make_async_copy(feat, x.at[pl.ds(2, 2), pl.ds(1, 2)], own_sem)
    own.start()
    loads = [
        pltpu.make_async_copy(src, dst, load_sem.at[i])
        for i, (src, dst) in enumerate(
            (
                (conv_in, w1), (down_proj, w2), (spatial_w, w3), (temporal_w, w4), (bias_in_h, bias_in),
                (bias_down_h, bias_down), (bias_mid_h, bias_mid), (gain_h, gain), (proj_h, proj_t),
            )
        )
    ]
    for load in loads:
        load.start()

    edge = jnp.zeros((PAD, x.shape[3]), F32)
    for c in range(3):
        for f in range(2):
            for o in range(2):
                acc[c, f, o, pl.ds(0, PAD), :] = edge
                acc[c, f, o, pl.ds(PAD + width, PAD), :] = edge
            acc2[c, f, pl.ds(0, PAD), :] = jnp.zeros((PAD, acc2.shape[3]), F32)
            acc2[c, f, pl.ds(PAD + lat, PAD), :] = jnp.zeros((PAD, acc2.shape[3]), F32)
    projs[...] = jnp.zeros(projs.shape, BF16)

    @pl.when(jnp.logical_not(has_prev))
    def _():
        x[pl.ds(0, 2)] = jnp.zeros((2,) + x.shape[1:], BF16)
        sp[pl.ds(0, 2)] = jnp.zeros((2,) + sp.shape[1:], BF16)

    @pl.when(jnp.logical_not(has_above))
    def _():
        for f in range(4):
            x[f, 0] = jnp.zeros(x.shape[2:], BF16)
        for f in range(2):
            act[f, 0] = jnp.zeros(act.shape[2:], BF16)

    @pl.when(jnp.logical_not(has_below))
    def _():
        for f in range(4):
            x[f, 3] = jnp.zeros(x.shape[2:], BF16)
        for f in range(2):
            act[f, 2] = jnp.zeros(act.shape[2:], BF16)

    def conv(f, frames, kept, first):
        for o in range(2):
            steps = [(n, n - f, b) for n in frames for b in kept[o]]
            lhs = jnp.concatenate([x[n, o + b] for n, a, b in steps], axis=-1)
            rhs = jnp.concatenate(
                [jnp.concatenate([w1[a, b, c] for c in range(3)], axis=-1) for n, a, b in steps], axis=0
            )
            total = jnp.dot(lhs, rhs, preferred_element_type=F32)
            for c in range(3):
                part = total[:, c * 128 : (c + 1) * 128]
                rows = (c, f, o, pl.ds(PAD, width))
                acc[rows] = part if first else acc[rows] + part

    held, halo = ((1, 2), (0, 1)), ((0,), (2,))
    own.wait()
    loads[0].wait()
    conv(0, (2,), held, True)
    conv(1, (2, 3), held, True)
    hear(0)

    both = jnp.logical_and
    relays = both(even, has_prev)
    passes = (has_next, even)
    for f in range(2):
        pl.when(has_prev)(to_next[1 - f].wait_recv)
        if f == 0:
            pl.when(both(relays, has_below))(relay_below.start)
            pl.when(both(relays, has_above))(relay_above.start)
        pl.when(has_above)(to_below[f].wait_recv)
        pl.when(both(passes[f], has_above))(pass_top[f].start)
        pl.when(has_below)(to_above[f].wait_recv)
        pl.when(both(passes[f], has_below))(pass_bottom[f].start)
    hear(1)
    conv(1, (1,), held, False)
    conv(1, (2, 3), halo, False)
    hear(2)
    conv(0, (0, 1), held, False)
    conv(0, (2,), halo, False)
    for load in loads[4:]:
        load.wait()
    for s in range(2 * per):
        projs[s, pl.ds(chans * s, chans), :] = proj_t[...]

    loads[1].wait()
    down_w = w2[...].reshape(4 * w2.shape[2], w2.shape[3])
    act_below = [remote(act.at[f, 1], act.at[f, 0], as_send.at[0, f], as_recv.at[0, f], "rows", below) for f in range(2)]
    act_above = [remote(act.at[f, 1], act.at[f, 2], as_send.at[1, f], as_recv.at[1, f], "rows", above) for f in range(2)]
    loads[2].wait()

    def spatial(f, b, first):
        weights = jnp.concatenate([w3[b, c] for c in range(3)], axis=-1)
        total = jnp.dot(act[f, b], weights, preferred_element_type=F32)
        size = w3.shape[3]
        for c in range(3):
            part = total[:, c * size : (c + 1) * size]
            rows = (c, f, pl.ds(PAD, lat))
            acc2[rows] = part if first else acc2[rows] + part

    for f in (1, 0):
        pl.when(both(has_prev, has_above))(pass_top[f].wait_recv)
        pl.when(both(has_prev, has_below))(pass_bottom[f].wait_recv)
        conv(f, tuple(range(f, 2)), halo, False)
        parts = []
        for o in range(2):
            for b in range(2):
                v = bias_in[...][None, :]
                for c in range(3):
                    v = v + acc[c, f, o, pl.ds(PAD - 1 + b + c, lat, stride=2), :]
                parts.append(silu(v).astype(BF16))
        d = jnp.dot(jnp.concatenate(parts, axis=-1), down_w, preferred_element_type=F32)
        d = (d + bias_down[...][None, :]).astype(BF16)
        down[f] = d
        act[f, 1] = silu(d.astype(F32)).astype(BF16)
        pl.when(has_below)(act_below[f].start)
        pl.when(has_above)(act_above[f].start)
        spatial(f, 1, True)

    hear(3)
    to_later = [remote(sp.at[2 + f], sp.at[f], ss_send.at[f], ss_recv.at[f], "tm", later) for f in range(2)]

    for f in (1, 0):
        pl.when(has_above)(act_below[f].wait_recv)
        spatial(f, 0, False)
        pl.when(has_below)(act_above[f].wait_recv)
        spatial(f, 2, False)
        v = acc2[0, f, pl.ds(PAD - 1, lat), :]
        for c in (1, 2):
            v = v + acc2[c, f, pl.ds(PAD - 1 + c, lat), :]
        sp[2 + f] = v.astype(BF16)
        pl.when(has_next)(to_later[f].start)

    loads[3].wait()

    def mixed(frame, step):
        return jnp.dot(sp[frame], w4[step], preferred_element_type=F32)

    local = [mixed(2, 2), mixed(3, 2) + mixed(2, 1)]
    half = normed.shape[3]
    total = None
    for f in (1, 0):
        pl.when(has_prev)(to_later[f].wait_recv)
        block = down[f].astype(F32) + bias_mid[...][None, :] + local[f]
        block = block + (mixed(0, 0) + mixed(1, 1) if f == 0 else mixed(1, 0))
        scale = lax.rsqrt(jnp.mean(block * block, axis=-1, keepdims=True) + 1e-06)
        value = block * scale * gain[...][None, :]
        for h in range(2):
            normed[f, h] = value[:, h * half : (h + 1) * half]
        for c in range(per):
            rows = jnp.concatenate(
                [normed[f, h, pl.ds(c, shards, stride=per), :] for h in range(2)], axis=-1
            ).astype(BF16)
            part = lax.dot_general(
                rows, projs[f * per + c], (((1,), (1,)), ((), ())), preferred_element_type=F32
            )
            total = part if total is None else total + part
    outbox[...] = total[:, None, :]

    hear(4)

    def token(peer, source):
        return remote(outbox.at[peer], inbox.at[source], a2a_send, a2a_recv, "rows", peer)

    middle = shards // 2
    token(lax.rem(row + middle, shards), row).start()

    def launch(k, carry):
        token(lax.rem(row + middle - k, shards), row).start()
        token(lax.rem(row + middle + k, shards), row).start()
        return carry

    lax.fori_loop(1, middle, launch, 0)
    inbox[row] = outbox[row]

    for f in range(2):
        pl.when(has_next)(to_next[f].wait_send)
        pl.when(has_next)(to_later[f].wait_send)
        for ok, copies in (
            (has_below, (to_below[f], act_below[f])),
            (has_above, (to_above[f], act_above[f])),
            (both(relays, has_below), (relay_below,) * f),
            (both(relays, has_above), (relay_above,) * f),
            (both(passes[f], has_above), (pass_top[f],)),
            (both(passes[f], has_below), (pass_bottom[f],)),
        ):
            for copy in copies:
                pl.when(ok)(copy.wait_send)

    others = pl.ds(0, shards - 1)
    pltpu.make_async_copy(outbox.at[others], inbox.at[others], a2a_recv).wait()
    out[...] = jnp.transpose(inbox[:, 0, :])[: 2 * per * chans, :]
    pltpu.make_async_copy(outbox.at[others], inbox.at[others], a2a_send).wait()


def shards_fn(
    sections, shards, features, conv_in, bias_in, down_proj, bias_down, spatial_w, temporal_w, bias_mid, norm_gain, latent_proj
):
    frames, height, width, c1 = features.shape
    lat, c2 = width // 2, down_proj.shape[3]
    chans = latent_proj.shape[1]
    per = lat // shards
    hbm = pl.BlockSpec(memory_space=pl.ANY)
    vmem = pl.BlockSpec(memory_space=pltpu.VMEM)
    dma = pltpu.SemaphoreType.DMA
    tokens = pl.pallas_call(
        functools.partial(kernel, sections, shards),
        out_shape=jax.ShapeDtypeStruct((frames * per * chans, shards), F32),
        in_specs=[hbm] * 10,
        out_specs=vmem,
        scratch_shapes=[
            pltpu.VMEM((4, 4, width, c1), BF16),
            pltpu.VMEM(conv_in.shape, BF16),
            pltpu.VMEM(down_proj.shape, BF16),
            pltpu.VMEM(spatial_w.shape, BF16),
            pltpu.VMEM(temporal_w.shape, BF16),
            pltpu.VMEM(bias_in.shape, F32),
            pltpu.VMEM(bias_down.shape, F32),
            pltpu.VMEM(bias_mid.shape, F32),
            pltpu.VMEM(norm_gain.shape, F32),
            pltpu.VMEM(latent_proj.shape[::-1], BF16),
            pltpu.VMEM((3, 2, 2, width + 2 * PAD, c1), F32),
            pltpu.VMEM((2, 3, lat, c2), BF16),
            pltpu.VMEM((3, 2, lat + 2 * PAD, c2), F32),
            pltpu.VMEM((4, lat, c2), BF16),
            pltpu.VMEM((2, lat, c2), BF16),
            pltpu.VMEM((2, 2, lat, c2 // 2), F32),
            pltpu.VMEM((2 * per, 128, c2), BF16),
            pltpu.VMEM((shards, 1, 128), F32),
            pltpu.VMEM((shards, 1, 128), F32),
            dma((9,)),
            dma,
            dma((7, 2)),
            dma((5, 2)),
            dma((2, 2)),
            dma((2, 2)),
            dma((2,)),
            dma((2,)),
            dma,
            dma,
            pltpu.SemaphoreType.REGULAR((8,)),
        ],
        compiler_params=pltpu.CompilerParams(collective_id=0, has_side_effects=True, vmem_limit_bytes=67_043_328),
        name="encoder",
    )(features, conv_in, bias_in, down_proj, bias_down, spatial_w, temporal_w, bias_mid, norm_gain, latent_proj.T)
    return tokens.reshape(frames, per, chans, shards)


def solution(mesh):
    sizes = mesh.shape
    return jax.shard_map(
        functools.partial(shards_fn, sizes["tm"], sizes["rows"]),
        mesh=mesh,
        in_specs=(P("tm", "rows", None, None), P(), P(), P(), P(), P(), P(), P(), P(), P()),
        out_specs=P("tm", "rows", None, None),
        check_vma=False,
    )
```

```python
import functools

import jax
import jax.numpy as jnp
from jax import lax
from jax.experimental import pallas as pl
from jax.experimental.pallas import tpu as pltpu
from jax.sharding import PartitionSpec as P

MESH = pl.DeviceIdType.MESH
F32 = jnp.float32
BF16 = jnp.bfloat16
PAD = 8


def silu(v):
    return v / (1.0 + jnp.exp(-v))


def remote(src, dst, send, recv, axis, peer):
    return pltpu.make_async_remote_copy(
        src_ref=src, dst_ref=dst, send_sem=send, recv_sem=recv, device_id={axis: peer}, device_id_type=MESH
    )


def kernel(
    sections, shards, feat, conv_in, bias_in_h, down_proj, bias_down_h, spatial_w, temporal_w, bias_mid_h, gain_h, proj_h, out,
    x, w1, w2, w3, w4, bias_in, bias_down, bias_mid, gain, proj_t, acc, act, acc2, sp, down, normed, projs, outbox, inbox,
    load_sem, own_sem, fs_send, fs_recv, as_send, as_recv, ss_send, ss_recv, a2a_send, a2a_recv, ready,
):
    tm, row = lax.axis_index("tm"), lax.axis_index("rows")
    width, lat = feat.shape[2], down.shape[1]
    chans = proj_t.shape[0]
    per = lat // shards
    above, below = lax.rem(row + shards - 1, shards), lax.rem(row + 1, shards)
    later, earlier = lax.rem(tm + 1, sections), lax.rem(tm + sections - 1, sections)
    even = lax.rem(tm, 2) == 0
    has_above, has_below = row > 0, row < shards - 1
    has_prev, has_next = tm > 0, tm < sections - 1

    barrier = pltpu.get_barrier_semaphore()
    for axis, peer in (("rows", above), ("rows", below), ("tm", later), ("tm", earlier)):
        pl.semaphore_signal(barrier, inc=1, device_id={axis: peer}, device_id_type=MESH)

    pl.semaphore_wait(barrier, 4)

    def pair(slot, frame):
        return fs_send.at[slot, frame], fs_recv.at[slot, frame]

    to_next = [remote(feat.at[f], x.at[f, pl.ds(1, 2)], *pair(2, f), "tm", later) for f in range(2)]
    to_below = [remote(feat.at[f, 1], x.at[2 + f, 0], *pair(0, f), "rows", below) for f in range(2)]
    to_above = [remote(feat.at[f, 0], x.at[2 + f, 3], *pair(1, f), "rows", above) for f in range(2)]
    relay_below = remote(x.at[1, 2], x.at[1, 0], *pair(3, 1), "rows", below)
    relay_above = remote(x.at[1, 1], x.at[1, 3], *pair(4, 1), "rows", above)
    pass_top = [remote(x.at[2 + f, 0], x.at[f, 0], fs_send.at[5, f], fs_recv.at[3, f], "tm", later) for f in range(2)]
    pass_bottom = [remote(x.at[2 + f, 3], x.at[f, 3], fs_send.at[6, f], fs_recv.at[4, f], "tm", later) for f in range(2)]

    for f in range(2):
        pl.when(has_next)(to_next[1 - f].start)
        pl.when(has_below)(to_below[f].start)
        pl.when(has_above)(to_above[f].start)

    rounds = []
    while 2 ** len(rounds) <= shards // 4:
        rounds.append(2 ** len(rounds))

    def tell(step):
        if step < len(rounds):
            for peer in (lax.rem(row + rounds[step], shards), lax.rem(row + shards - rounds[step], shards)):
                pl.semaphore_signal(ready.at[step], inc=1, device_id={"rows": peer}, device_id_type=MESH)

    def hear(step):
        if step < len(rounds):
            pl.semaphore_wait(ready.at[step], 2)
            tell(step + 1)

    tell(0)

    own = pltpu.make_async_copy(feat, x.at[pl.ds(2, 2), pl.ds(1, 2)], own_sem)
    own.start()
    loads = [
        pltpu.make_async_copy(src, dst, load_sem.at[i])
        for i, (src, dst) in enumerate(
            (
                (conv_in, w1), (down_proj, w2), (spatial_w, w3), (temporal_w, w4), (bias_in_h, bias_in),
                (bias_down_h, bias_down), (bias_mid_h, bias_mid), (gain_h, gain), (proj_h, proj_t),
            )
        )
    ]
    for load in loads:
        load.start()

    edge = jnp.zeros((PAD, x.shape[3]), F32)
    for c in range(3):
        for f in range(2):
            for o in range(2):
                acc[c, f, o, pl.ds(0, PAD), :] = edge
                acc[c, f, o, pl.ds(PAD + width, PAD), :] = edge
            acc2[c, f, pl.ds(0, PAD), :] = jnp.zeros((PAD, acc2.shape[3]), F32)
            acc2[c, f, pl.ds(PAD + lat, PAD), :] = jnp.zeros((PAD, acc2.shape[3]), F32)
    projs[...] = jnp.zeros(projs.shape, BF16)

    @pl.when(jnp.logical_not(has_prev))
    def _():
        x[pl.ds(0, 2)] = jnp.zeros((2,) + x.shape[1:], BF16)
        sp[pl.ds(0, 2)] = jnp.zeros((2,) + sp.shape[1:], BF16)

    @pl.when(jnp.logical_not(has_above))
    def _():
        for f in range(4):
            x[f, 0] = jnp.zeros(x.shape[2:], BF16)
        for f in range(2):
            act[f, 0] = jnp.zeros(act.shape[2:], BF16)

    @pl.when(jnp.logical_not(has_below))
    def _():
        for f in range(4):
            x[f, 3] = jnp.zeros(x.shape[2:], BF16)
        for f in range(2):
            act[f, 2] = jnp.zeros(act.shape[2:], BF16)

    def conv(f, frames, kept, first):
        for o in range(2):
            steps = [(n, n - f, b) for n in frames for b in kept[o]]
            lhs = jnp.concatenate([x[n, o + b] for n, a, b in steps], axis=-1)
            rhs = jnp.concatenate(
                [jnp.concatenate([w1[a, b, c] for c in range(3)], axis=-1) for n, a, b in steps], axis=0
            )
            total = jnp.dot(lhs, rhs, preferred_element_type=F32)
            for c in range(3):
                part = total[:, c * 128 : (c + 1) * 128]
                rows = (c, f, o, pl.ds(PAD, width))
                acc[rows] = part if first else acc[rows] + part

    held, halo = ((1, 2), (0, 1)), ((0,), (2,))
    own.wait()
    loads[0].wait()
    conv(0, (2,), held, True)
    conv(1, (2, 3), held, True)
    hear(0)

    both = jnp.logical_and
    relays = both(even, has_prev)
    passes = (has_next, even)
    for f in range(2):
        pl.when(has_prev)(to_next[1 - f].wait_recv)
        if f == 0:
            pl.when(both(relays, has_below))(relay_below.start)
            pl.when(both(relays, has_above))(relay_above.start)
        pl.when(has_above)(to_below[f].wait_recv)
        pl.when(both(passes[f], has_above))(pass_top[f].start)
        pl.when(has_below)(to_above[f].wait_recv)
        pl.when(both(passes[f], has_below))(pass_bottom[f].start)
    hear(1)
    conv(1, (1,), held, False)
    conv(1, (2, 3), halo, False)
    for i in (1, 4, 5):
        loads[i].wait()
    down_w = w2[...].reshape(4 * w2.shape[2], w2.shape[3])
    act_below = [remote(act.at[f, 1], act.at[f, 0], as_send.at[0, f], as_recv.at[0, f], "rows", below) for f in range(2)]
    act_above = [remote(act.at[f, 1], act.at[f, 2], as_send.at[1, f], as_recv.at[1, f], "rows", above) for f in range(2)]

    def spatial(f, b, first):
        weights = jnp.concatenate([w3[b, c] for c in range(3)], axis=-1)
        total = jnp.dot(act[f, b], weights, preferred_element_type=F32)
        size = w3.shape[3]
        for c in range(3):
            part = total[:, c * size : (c + 1) * size]
            rows = (c, f, pl.ds(PAD, lat))
            acc2[rows] = part if first else acc2[rows] + part

    for f in (1, 0):
        if f == 0:
            conv(0, (0, 1), held, False)
        pl.when(both(has_prev, has_above))(pass_top[f].wait_recv)
        pl.when(both(has_prev, has_below))(pass_bottom[f].wait_recv)
        conv(f, (1,) if f == 1 else (0, 1, 2), halo, False)
        parts = []
        for o in range(2):
            for b in range(2):
                v = bias_in[...][None, :]
                for c in range(3):
                    v = v + acc[c, f, o, pl.ds(PAD - 1 + b + c, lat, stride=2), :]
                parts.append(silu(v).astype(BF16))
        d = jnp.dot(jnp.concatenate(parts, axis=-1), down_w, preferred_element_type=F32)
        d = (d + bias_down[...][None, :]).astype(BF16)
        down[f] = d
        act[f, 1] = silu(d.astype(F32)).astype(BF16)
        pl.when(has_below)(act_below[f].start)
        pl.when(has_above)(act_above[f].start)
        if f == 1:
            hear(2)
            loads[2].wait()
            spatial(1, 1, True)

    spatial(0, 1, True)
    hear(3)
    for i in (6, 7, 8):
        loads[i].wait()
    for s in range(2 * per):
        projs[s, pl.ds(chans * s, chans), :] = proj_t[...]
    to_later = [remote(sp.at[2 + f], sp.at[f], ss_send.at[f], ss_recv.at[f], "tm", later) for f in range(2)]

    for f in (1, 0):
        pl.when(has_above)(act_below[f].wait_recv)
        spatial(f, 0, False)
        pl.when(has_below)(act_above[f].wait_recv)
        spatial(f, 2, False)
        v = acc2[0, f, pl.ds(PAD - 1, lat), :]
        for c in (1, 2):
            v = v + acc2[c, f, pl.ds(PAD - 1 + c, lat), :]
        sp[2 + f] = v.astype(BF16)
        pl.when(has_next)(to_later[f].start)

    loads[3].wait()

    def mixed(frame, step):
        return jnp.dot(sp[frame], w4[step], preferred_element_type=F32)

    local = [mixed(2, 2), mixed(3, 2) + mixed(2, 1)]
    half = normed.shape[3]
    total = None
    for f in (1, 0):
        pl.when(has_prev)(to_later[f].wait_recv)
        block = down[f].astype(F32) + bias_mid[...][None, :] + local[f]
        block = block + (mixed(0, 0) + early if f == 0 else mixed(1, 0))
        scale = lax.rsqrt(jnp.mean(block * block, axis=-1, keepdims=True) + 1e-06)
        value = block * scale * gain[...][None, :]
        early = mixed(1, 1) if f == 1 else None
        for h in range(2):
            normed[f, h] = value[:, h * half : (h + 1) * half]
        for c in range(per):
            rows = jnp.concatenate(
                [normed[f, h, pl.ds(c, shards, stride=per), :] for h in range(2)], axis=-1
            ).astype(BF16)
            part = lax.dot_general(
                rows, projs[f * per + c], (((1,), (1,)), ((), ())), preferred_element_type=F32
            )
            total = part if total is None else total + part
    outbox[...] = total[:, None, :]

    hear(4)

    def token(peer, source):
        return remote(outbox.at[peer], inbox.at[source], a2a_send, a2a_recv, "rows", peer)

    middle = shards // 2
    token(lax.rem(row + middle, shards), row).start()

    def launch(k, carry):
        token(lax.rem(row + middle - k, shards), row).start()
        token(lax.rem(row + middle + k, shards), row).start()
        return carry

    lax.fori_loop(1, middle, launch, 0)
    inbox[row] = outbox[row]

    for f in range(2):
        pl.when(has_next)(to_next[f].wait_send)
        pl.when(has_next)(to_later[f].wait_send)
        for ok, copies in (
            (has_below, (to_below[f], act_below[f])),
            (has_above, (to_above[f], act_above[f])),
            (both(relays, has_below), (relay_below,) * f),
            (both(relays, has_above), (relay_above,) * f),
            (both(passes[f], has_above), (pass_top[f],)),
            (both(passes[f], has_below), (pass_bottom[f],)),
        ):
            for copy in copies:
                pl.when(ok)(copy.wait_send)

    others = pl.ds(0, shards - 1)
    pltpu.make_async_copy(outbox.at[others], inbox.at[others], a2a_recv).wait()
    out[...] = jnp.transpose(inbox[:, 0, :])[: 2 * per * chans, :]
    pltpu.make_async_copy(outbox.at[others], inbox.at[others], a2a_send).wait()


def shards_fn(
    sections, shards, features, conv_in, bias_in, down_proj, bias_down, spatial_w, temporal_w, bias_mid, norm_gain, latent_proj
):
    frames, height, width, c1 = features.shape
    lat, c2 = width // 2, down_proj.shape[3]
    chans = latent_proj.shape[1]
    per = lat // shards
    hbm = pl.BlockSpec(memory_space=pl.ANY)
    vmem = pl.BlockSpec(memory_space=pltpu.VMEM)
    dma = pltpu.SemaphoreType.DMA
    tokens = pl.pallas_call(
        functools.partial(kernel, sections, shards),
        out_shape=jax.ShapeDtypeStruct((frames * per * chans, shards), F32),
        in_specs=[hbm] * 10,
        out_specs=vmem,
        scratch_shapes=[
            pltpu.VMEM((4, 4, width, c1), BF16),
            pltpu.VMEM(conv_in.shape, BF16),
            pltpu.VMEM(down_proj.shape, BF16),
            pltpu.VMEM(spatial_w.shape, BF16),
            pltpu.VMEM(temporal_w.shape, BF16),
            pltpu.VMEM(bias_in.shape, F32),
            pltpu.VMEM(bias_down.shape, F32),
            pltpu.VMEM(bias_mid.shape, F32),
            pltpu.VMEM(norm_gain.shape, F32),
            pltpu.VMEM(latent_proj.shape[::-1], BF16),
            pltpu.VMEM((3, 2, 2, width + 2 * PAD, c1), F32),
            pltpu.VMEM((2, 3, lat, c2), BF16),
            pltpu.VMEM((3, 2, lat + 2 * PAD, c2), F32),
            pltpu.VMEM((4, lat, c2), BF16),
            pltpu.VMEM((2, lat, c2), BF16),
            pltpu.VMEM((2, 2, lat, c2 // 2), F32),
            pltpu.VMEM((2 * per, 128, c2), BF16),
            pltpu.VMEM((shards, 1, 128), F32),
            pltpu.VMEM((shards, 1, 128), F32),
            dma((9,)),
            dma,
            dma((7, 2)),
            dma((5, 2)),
            dma((2, 2)),
            dma((2, 2)),
            dma((2,)),
            dma((2,)),
            dma,
            dma,
            pltpu.SemaphoreType.REGULAR((8,)),
        ],
        compiler_params=pltpu.CompilerParams(collective_id=0, has_side_effects=True, vmem_limit_bytes=67_043_328),
        name="encoder",
    )(features, conv_in, bias_in, down_proj, bias_down, spatial_w, temporal_w, bias_mid, norm_gain, latent_proj.T)
    return tokens.reshape(frames, per, chans, shards)


def solution(mesh):
    sizes = mesh.shape
    return jax.shard_map(
        functools.partial(shards_fn, sizes["tm"], sizes["rows"]),
        mesh=mesh,
        in_specs=(P("tm", "rows", None, None), P(), P(), P(), P(), P(), P(), P(), P(), P()),
        out_specs=P("tm", "rows", None, None),
        check_vma=False,
    )
```

```python
import functools

import jax
import jax.numpy as jnp
from jax import lax
from jax.experimental import pallas as pl
from jax.experimental.pallas import tpu as pltpu
from jax.sharding import PartitionSpec as P

MESH = pl.DeviceIdType.MESH
F32 = jnp.float32
BF16 = jnp.bfloat16
PAD = 8


def silu(v):
    return v / (1.0 + jnp.exp(-v))


def remote(src, dst, send, recv, axis, peer):
    return pltpu.make_async_remote_copy(
        src_ref=src, dst_ref=dst, send_sem=send, recv_sem=recv, device_id={axis: peer}, device_id_type=MESH
    )


def kernel(
    sections, shards, feat, conv_in, bias_in_h, down_proj, bias_down_h, spatial_w, temporal_w, bias_mid_h, gain_h, proj_h, out,
    x, w1, w2, w3, w4, bias_in, bias_down, bias_mid, gain, proj_t, acc, act, acc2, sp, down, normed, projs, outbox, inbox,
    load_sem, own_sem, fs_send, fs_recv, as_send, as_recv, ss_send, ss_recv, a2a_send, a2a_recv, ready,
):
    tm, row = lax.axis_index("tm"), lax.axis_index("rows")
    width, lat = feat.shape[2], down.shape[1]
    chans = proj_t.shape[0]
    per = lat // shards
    above, below = lax.rem(row + shards - 1, shards), lax.rem(row + 1, shards)
    later, earlier = lax.rem(tm + 1, sections), lax.rem(tm + sections - 1, sections)
    even = lax.rem(tm, 2) == 0
    has_above, has_below = row > 0, row < shards - 1
    has_prev, has_next = tm > 0, tm < sections - 1

    barrier = pltpu.get_barrier_semaphore()
    for axis, peer in (("rows", above), ("rows", below), ("tm", later), ("tm", earlier)):
        pl.semaphore_signal(barrier, inc=1, device_id={axis: peer}, device_id_type=MESH)

    pl.semaphore_wait(barrier, 4)

    def pair(slot, frame):
        return fs_send.at[slot, frame], fs_recv.at[slot, frame]

    to_next = [remote(feat.at[f], x.at[f, pl.ds(1, 2)], *pair(2, f), "tm", later) for f in range(2)]
    to_below = [remote(feat.at[f, 1], x.at[2 + f, 0], *pair(0, f), "rows", below) for f in range(2)]
    to_above = [remote(feat.at[f, 0], x.at[2 + f, 3], *pair(1, f), "rows", above) for f in range(2)]
    relay_below = remote(x.at[1, 2], x.at[1, 0], *pair(3, 1), "rows", below)
    relay_above = remote(x.at[1, 1], x.at[1, 3], *pair(4, 1), "rows", above)
    pass_top = [remote(x.at[2 + f, 0], x.at[f, 0], fs_send.at[5, f], fs_recv.at[3, f], "tm", later) for f in range(2)]
    pass_bottom = [remote(x.at[2 + f, 3], x.at[f, 3], fs_send.at[6, f], fs_recv.at[4, f], "tm", later) for f in range(2)]

    for f in range(2):
        pl.when(has_next)(to_next[1 - f].start)
        pl.when(has_below)(to_below[f].start)
        pl.when(has_above)(to_above[f].start)

    rounds = []
    while 2 ** len(rounds) <= shards // 4:
        rounds.append(2 ** len(rounds))

    def tell(step):
        if step < len(rounds):
            for peer in (lax.rem(row + rounds[step], shards), lax.rem(row + shards - rounds[step], shards)):
                pl.semaphore_signal(ready.at[step], inc=1, device_id={"rows": peer}, device_id_type=MESH)

    def hear(step):
        if step < len(rounds):
            pl.semaphore_wait(ready.at[step], 2)
            tell(step + 1)

    tell(0)

    own = pltpu.make_async_copy(feat, x.at[pl.ds(2, 2), pl.ds(1, 2)], own_sem)
    own.start()
    loads = [
        pltpu.make_async_copy(src, dst, load_sem.at[i])
        for i, (src, dst) in enumerate(
            (
                (conv_in, w1), (down_proj, w2), (spatial_w, w3), (temporal_w, w4), (bias_in_h, bias_in),
                (bias_down_h, bias_down), (bias_mid_h, bias_mid), (gain_h, gain), (proj_h, proj_t),
            )
        )
    ]
    for load in loads:
        load.start()

    edge = jnp.zeros((PAD, x.shape[3]), F32)
    for c in range(3):
        for f in range(2):
            for o in range(2):
                acc[c, f, o, pl.ds(0, PAD), :] = edge
                acc[c, f, o, pl.ds(PAD + width, PAD), :] = edge
            acc2[c, f, pl.ds(0, PAD), :] = jnp.zeros((PAD, acc2.shape[3]), F32)
            acc2[c, f, pl.ds(PAD + lat, PAD), :] = jnp.zeros((PAD, acc2.shape[3]), F32)
    projs[...] = jnp.zeros(projs.shape, BF16)

    @pl.when(jnp.logical_not(has_prev))
    def _():
        x[pl.ds(0, 2)] = jnp.zeros((2,) + x.shape[1:], BF16)
        sp[pl.ds(0, 2)] = jnp.zeros((2,) + sp.shape[1:], BF16)

    @pl.when(jnp.logical_not(has_above))
    def _():
        for f in range(4):
            x[f, 0] = jnp.zeros(x.shape[2:], BF16)
        for f in range(2):
            act[f, 0] = jnp.zeros(act.shape[2:], BF16)

    @pl.when(jnp.logical_not(has_below))
    def _():
        for f in range(4):
            x[f, 3] = jnp.zeros(x.shape[2:], BF16)
        for f in range(2):
            act[f, 2] = jnp.zeros(act.shape[2:], BF16)

    def conv(f, frames, kept, first):
        for o in range(2):
            steps = [(n, n - f, b) for n in frames for b in kept[o]]
            lhs = jnp.concatenate([x[n, o + b] for n, a, b in steps], axis=-1)
            rhs = jnp.concatenate(
                [jnp.concatenate([w1[a, b, c] for c in range(3)], axis=-1) for n, a, b in steps], axis=0
            )
            total = jnp.dot(lhs, rhs, preferred_element_type=F32)
            for c in range(3):
                part = total[:, c * 128 : (c + 1) * 128]
                rows = (c, f, o, pl.ds(PAD, width))
                acc[rows] = part if first else acc[rows] + part

    held, halo = ((1, 2), (0, 1)), ((0,), (2,))
    own.wait()
    loads[0].wait()
    conv(0, (2,), held, True)
    conv(1, (2, 3), held, True)
    hear(0)

    both = jnp.logical_and
    relays = both(even, has_prev)
    passes = (has_next, even)
    for f in range(2):
        pl.when(has_prev)(to_next[1 - f].wait_recv)
        if f == 0:
            pl.when(both(relays, has_below))(relay_below.start)
            pl.when(both(relays, has_above))(relay_above.start)
        pl.when(has_above)(to_below[f].wait_recv)
        pl.when(both(passes[f], has_above))(pass_top[f].start)
        pl.when(has_below)(to_above[f].wait_recv)
        pl.when(both(passes[f], has_below))(pass_bottom[f].start)
    hear(1)
    conv(1, (1,), held, False)
    conv(1, (2, 3), halo, False)
    hear(2)
    conv(0, (0, 1), held, False)
    conv(0, (2,), halo, False)
    for load in loads[4:]:
        load.wait()
    for s in range(2 * per):
        projs[s, pl.ds(chans * s, chans), :] = proj_t[...]

    loads[1].wait()
    down_w = w2[...].reshape(4 * w2.shape[2], w2.shape[3])
    act_below = [remote(act.at[f, 1], act.at[f, 0], as_send.at[0, f], as_recv.at[0, f], "rows", below) for f in range(2)]
    act_above = [remote(act.at[f, 1], act.at[f, 2], as_send.at[1, f], as_recv.at[1, f], "rows", above) for f in range(2)]
    loads[2].wait()

    def spatial(f, b, first):
        weights = jnp.concatenate([w3[b, c] for c in range(3)], axis=-1)
        total = jnp.dot(act[f, b], weights, preferred_element_type=F32)
        size = w3.shape[3]
        for c in range(3):
            part = total[:, c * size : (c + 1) * size]
            rows = (c, f, pl.ds(PAD, lat))
            acc2[rows] = part if first else acc2[rows] + part

    for f in (1, 0):
        pl.when(both(has_prev, has_above))(pass_top[f].wait_recv)
        pl.when(both(has_prev, has_below))(pass_bottom[f].wait_recv)
        conv(f, tuple(range(f, 2)), halo, False)
        parts = []
        for o in range(2):
            for b in range(2):
                v = bias_in[...][None, :]
                for c in range(3):
                    v = v + acc[c, f, o, pl.ds(PAD - 1 + b + c, lat, stride=2), :]
                parts.append(silu(v).astype(BF16))
        d = jnp.dot(jnp.concatenate(parts, axis=-1), down_w, preferred_element_type=F32)
        d = (d + bias_down[...][None, :]).astype(BF16)
        down[f] = d
        act[f, 1] = silu(d.astype(F32)).astype(BF16)
        pl.when(has_below)(act_below[f].start)
        pl.when(has_above)(act_above[f].start)
        spatial(f, 1, True)

    hear(3)
    to_later = [remote(sp.at[2 + f], sp.at[f], ss_send.at[f], ss_recv.at[f], "tm", later) for f in range(2)]

    for f in (1, 0):
        pl.when(has_above)(act_below[f].wait_recv)
        spatial(f, 0, False)
        pl.when(has_below)(act_above[f].wait_recv)
        spatial(f, 2, False)
        v = acc2[0, f, pl.ds(PAD - 1, lat), :]
        for c in (1, 2):
            v = v + acc2[c, f, pl.ds(PAD - 1 + c, lat), :]
        sp[2 + f] = v.astype(BF16)
        pl.when(has_next)(to_later[f].start)

    loads[3].wait()

    def mixed(frame, step):
        return jnp.dot(sp[frame], w4[step], preferred_element_type=F32)

    local = [mixed(2, 2), mixed(3, 2) + mixed(2, 1)]
    half = normed.shape[3]
    total = None
    for f in (1, 0):
        pl.when(has_prev)(to_later[f].wait_recv)
        block = down[f].astype(F32) + bias_mid[...][None, :] + local[f]
        block = block + (mixed(0, 0) + mixed(1, 1) if f == 0 else mixed(1, 0))
        scale = lax.rsqrt(jnp.mean(block * block, axis=-1, keepdims=True) + 1e-06)
        value = block * scale * gain[...][None, :]
        for h in range(2):
            normed[f, h] = value[:, h * half : (h + 1) * half]
        for c in range(per):
            rows = jnp.concatenate(
                [normed[f, h, pl.ds(c, shards, stride=per), :] for h in range(2)], axis=-1
            ).astype(BF16)
            part = lax.dot_general(
                rows, projs[f * per + c], (((1,), (1,)), ((), ())), preferred_element_type=F32
            )
            total = part if total is None else total + part
    outbox[...] = total[:, None, :]

    hear(4)

    def token(peer, source):
        return remote(outbox.at[peer], inbox.at[source], a2a_send, a2a_recv, "rows", peer)

    middle = shards // 2
    token(lax.rem(row + middle, shards), row).start()

    def launch(k, carry):
        token(lax.rem(row + middle - k, shards), row).start()
        token(lax.rem(row + middle + k, shards), row).start()
        return carry

    lax.fori_loop(1, middle, launch, 0)
    inbox[row] = outbox[row]

    for f in range(2):
        pl.when(has_next)(to_next[f].wait_send)
        pl.when(has_next)(to_later[f].wait_send)
        for ok, copies in (
            (has_below, (to_below[f], act_below[f])),
            (has_above, (to_above[f], act_above[f])),
            (both(relays, has_below), (relay_below,) * f),
            (both(relays, has_above), (relay_above,) * f),
            (both(passes[f], has_above), (pass_top[f],)),
            (both(passes[f], has_below), (pass_bottom[f],)),
        ):
            for copy in copies:
                pl.when(ok)(copy.wait_send)

    others = pl.ds(0, shards - 1)
    pltpu.make_async_copy(outbox.at[others], inbox.at[others], a2a_recv).wait()
    out[...] = inbox[:, 0, :]
    pltpu.make_async_copy(outbox.at[others], inbox.at[others], a2a_send).wait()


def shards_fn(
    sections, shards, features, conv_in, bias_in, down_proj, bias_down, spatial_w, temporal_w, bias_mid, norm_gain, latent_proj
):
    frames, height, width, c1 = features.shape
    lat, c2 = width // 2, down_proj.shape[3]
    chans = latent_proj.shape[1]
    per = lat // shards
    hbm = pl.BlockSpec(memory_space=pl.ANY)
    vmem = pl.BlockSpec(memory_space=pltpu.VMEM)
    dma = pltpu.SemaphoreType.DMA
    tokens = pl.pallas_call(
        functools.partial(kernel, sections, shards),
        out_shape=jax.ShapeDtypeStruct((shards, 128), F32),
        in_specs=[hbm] * 10,
        out_specs=vmem,
        scratch_shapes=[
            pltpu.VMEM((4, 4, width, c1), BF16),
            pltpu.VMEM(conv_in.shape, BF16),
            pltpu.VMEM(down_proj.shape, BF16),
            pltpu.VMEM(spatial_w.shape, BF16),
            pltpu.VMEM(temporal_w.shape, BF16),
            pltpu.VMEM(bias_in.shape, F32),
            pltpu.VMEM(bias_down.shape, F32),
            pltpu.VMEM(bias_mid.shape, F32),
            pltpu.VMEM(norm_gain.shape, F32),
            pltpu.VMEM(latent_proj.shape[::-1], BF16),
            pltpu.VMEM((3, 2, 2, width + 2 * PAD, c1), F32),
            pltpu.VMEM((2, 3, lat, c2), BF16),
            pltpu.VMEM((3, 2, lat + 2 * PAD, c2), F32),
            pltpu.VMEM((4, lat, c2), BF16),
            pltpu.VMEM((2, lat, c2), BF16),
            pltpu.VMEM((2, 2, lat, c2 // 2), F32),
            pltpu.VMEM((2 * per, 128, c2), BF16),
            pltpu.VMEM((shards, 1, 128), F32),
            pltpu.VMEM((shards, 1, 128), F32),
            dma((9,)),
            dma,
            dma((7, 2)),
            dma((5, 2)),
            dma((2, 2)),
            dma((2, 2)),
            dma((2,)),
            dma((2,)),
            dma,
            dma,
            pltpu.SemaphoreType.REGULAR((8,)),
        ],
        compiler_params=pltpu.CompilerParams(collective_id=0, has_side_effects=True, vmem_limit_bytes=67_043_328),
        name="encoder",
    )(features, conv_in, bias_in, down_proj, bias_down, spatial_w, temporal_w, bias_mid, norm_gain, latent_proj.T)
    return tokens[:, : frames * per * chans].T.reshape(frames, per, chans, shards)


def solution(mesh):
    sizes = mesh.shape
    return jax.shard_map(
        functools.partial(shards_fn, sizes["tm"], sizes["rows"]),
        mesh=mesh,
        in_specs=(P("tm", "rows", None, None), P(), P(), P(), P(), P(), P(), P(), P(), P()),
        out_specs=P("tm", "rows", None, None),
        check_vma=False,
    )
```
